256 devices in a mesh: leaf: 32 (over z, y), col: 8 (over x, core).
Axes of the slice: x: 4, y: 4, z: 8, core: 2. Of those that a mesh axis runs over, the one named last changes fastest.
Arguments:
- row_factors: bfloat16 [128, 512, 128], P('leaf', 'col'), may hold values from -0.25 to 0.25
- col_factors: bfloat16 [128, 512, 128], P('col', 'leaf'), may hold values from -0.25 to 0.25
- far_cols: int32 [128, 32], P('leaf', 'col'), may hold values from 0 to 127, as said below
- far_coupling: bfloat16 [128, 32, 64, 64], P('leaf', 'col'), may hold values from -0.75 to 0.75
- row_transfer: bfloat16 [128, 64, 64], P('leaf'), may hold values from -0.75 to 0.75
- col_transfer: bfloat16 [128, 64, 64], P('col'), may hold values from -0.75 to 0.75
- par_cols: int32 [64, 16], P('leaf', 'col'), may hold values from 0 to 63, as said below
- par_coupling: bfloat16 [64, 16, 64, 64], P('leaf', 'col'), may hold values from -0.75 to 0.75
- near_pattern: int32 [5120, 2], P(('leaf', 'col')), may hold values from -1 to 127, as said below
- near_blocks: bfloat16 [5120, 512, 512], P(('leaf', 'col')), may hold values from -0.25 to 0.25
- probes: bfloat16 [128, 512, 256], P('col', 'leaf'), may hold values from -6 to 6
Outputs:
- new_basis: bfloat16 [128, 512, 64], P('leaf', 'col')
- parent_transfer: float32 [64, 128, 64], P('leaf')
- near_image: float32 [128, 512, 256], P('leaf', 'col')
The draws below stay inside these ranges and needn't reach their ends.
Inputs may be any that keep to these rules, and one draw needn't show every extreme that they name: `far_cols`: in every row, entries k * 4 to (k + 1) * 4 - 1 are distinct column clusters between k * 16 and (k + 1) * 16 - 1. `par_cols`: in every row, entries k * 2 to (k + 1) * 2 - 1 are distinct column parents between k * 8 and (k + 1) * 8 - 1. `near_pattern`: slots come in aligned blocks of 20. In block b, with i = b // 8 and j = b % 8, every used slot names a row cluster between i * 4 and (i + 1) * 4 - 1 and a column cluster between j * 16 and (j + 1) * 16 - 1, no pair twice; used slots come first in a block, unused slots hold -1 in both entries; in every draw some block is full.
All inputs are finite; a program needn't handle non-finite values.
Results may differ from the reference program's by a relative error of at most 0.015.
Values may be sent and summed in bfloat16 or wider, within the bound.
No kernel may reach another device: no remote copies, remote signals or barrier semaphores. Data moves between devices by JAX's collectives and lax.ppermute only.
A program may use at most 128 MiB of HBM per device.

```python
import jax
import jax.numpy as jnp
from jax import lax

LEAF = 512
RANK = 64
PROBES = 256
FAR_ROW = 4
PAR_ROW = 2
SWEEPS = 3
LEAF_DEV = 4
NEAR_DEV = 20
EXT = 128
NLEAF = 128
NPAR = 64
COL_DEV = 16
FAR_COLS = 32
PAR_COLS = 16
NEAR_SLOTS = 5120


def pick_distinct(key, leading, choices, taken):
    scores = jax.random.randint(key, leading + (choices,), 0, 1 << 20) * choices + jnp.arange(choices)
    return jnp.argsort(scores, axis=-1)[..., :taken]


def draw_far_cols(key, part):
    shards = NLEAF // COL_DEV
    picked = pick_distinct(jax.random.fold_in(key, 11), (NLEAF, shards), COL_DEV, FAR_ROW)
    placed = picked + (jnp.arange(shards) * COL_DEV)[None, :, None]
    return placed.reshape(NLEAF, shards * FAR_ROW).astype(jnp.int32)


def draw_par_cols(key, part):
    shards = NLEAF // COL_DEV
    parents_shard = COL_DEV // 2
    picked = pick_distinct(jax.random.fold_in(key, 13), (NPAR, shards), parents_shard, PAR_ROW)
    placed = picked + (jnp.arange(shards) * parents_shard)[None, :, None]
    return placed.reshape(NPAR, shards * PAR_ROW).astype(jnp.int32)


def draw_near_pattern(key, part):
    devices = NEAR_SLOTS // NEAR_DEV
    shards = NLEAF // COL_DEV
    pair_count = LEAF_DEV * COL_DEV
    key_count = jax.random.fold_in(key, 21)
    key_filled = jax.random.fold_in(key, 22)
    key_single = jax.random.fold_in(key, 23)
    key_pairs = jax.random.fold_in(key, 24)
    counts = jax.random.randint(key_count, (devices,), max(1, NEAR_DEV // 8), NEAR_DEV // 2 + 1)
    filled = jax.random.randint(key_filled, (devices,), 0, 8) == 0
    filled = filled | (jnp.arange(devices) == jax.random.randint(key_single, (), 0, devices))
    counts = jnp.where(filled, NEAR_DEV, counts)
    picked = pick_distinct(key_pairs, (devices,), pair_count, NEAR_DEV)
    device_ids = jnp.arange(devices)[:, None]
    row_ids = device_ids // shards * LEAF_DEV + picked // COL_DEV
    col_ids = device_ids % shards * COL_DEV + picked % COL_DEV
    in_use = jnp.arange(NEAR_DEV)[None, :] < counts[:, None]
    row_ids = jnp.where(in_use, row_ids, -1)
    col_ids = jnp.where(in_use, col_ids, -1)
    return jnp.stack([row_ids, col_ids], axis=-1).reshape(NEAR_SLOTS, 2).astype(jnp.int32)


def block_scale(own_key, shape, cuts, low, high):
    gain, own = 1.0, jax.random.fold_in(own_key, 6)
    for axis_at, shards_of in cuts:
        heights = jnp.exp(jax.random.uniform(jax.random.fold_in(own, axis_at), (shards_of,), jnp.float32, low / len(cuts), high / len(cuts)))
        gain = gain * jnp.repeat(heights, shape[axis_at] // shards_of).reshape([-1 if axis == axis_at else 1 for axis in range(len(shape))])
    return gain


def gaussian(key, dims, scale, bound, cuts=(), kind=jnp.bfloat16):
    level = block_scale(key, dims, cuts, -0.22, 0.18) if cuts else 1.0
    array = jax.random.normal(key, dims, jnp.float32) * scale * level
    return jnp.minimum(jnp.maximum(array, -bound), bound).astype(kind)


def setup_inputs(seed: int = 0) -> dict:
    splits = jax.random.split(jax.random.key(seed), 12)
    return {
        "row_factors": gaussian(splits[0], (NLEAF, LEAF, EXT), LEAF ** -0.5, 0.25, ((0, 32), (1, 8))),
        "col_factors": gaussian(splits[1], (NLEAF, LEAF, EXT), LEAF ** -0.5, 0.25, ((0, 8), (1, 32))),
        "far_cols": draw_far_cols(jax.random.fold_in(splits[11], 71), 0),
        "far_coupling": gaussian(splits[3], (NLEAF, FAR_COLS, RANK, RANK), RANK ** -0.5, 0.75, ((0, 32), (1, 8))),
        "row_transfer": gaussian(splits[4], (NLEAF, RANK, RANK), RANK ** -0.5, 0.75, ((0, 32),)),
        "col_transfer": gaussian(splits[5], (NLEAF, RANK, RANK), RANK ** -0.5, 0.75, ((0, 8),)),
        "par_cols": draw_par_cols(jax.random.fold_in(splits[11], 71), 0),
        "par_coupling": gaussian(splits[7], (NPAR, PAR_COLS, RANK, RANK), RANK ** -0.5, 0.75, ((0, 32), (1, 8))),
        "near_pattern": draw_near_pattern(jax.random.fold_in(splits[11], 71), 0),
        "near_blocks": gaussian(splits[9], (NEAR_SLOTS, LEAF, LEAF), LEAF ** -0.5, 0.25, ((0, 256),)),
        "probes": gaussian(splits[10], (NLEAF, LEAF, PROBES), 1.0, 6.0, ((0, 8), (1, 32))),
    }


HIGHEST = lax.Precision.HIGHEST

def matmul_exact(left, right):
    return jnp.matmul(left, right, precision=HIGHEST)

def transpose_last(matrix):
    return jnp.swapaxes(matrix, -1, -2)

def assemble(upper_left, crosswise, lower_right):
    upper = jnp.concatenate([upper_left, crosswise], axis=-1)
    lower = jnp.concatenate([transpose_last(crosswise), lower_right], axis=-1)
    return jnp.concatenate([upper, lower], axis=-2)

def couple_block(coupling, gram):
    columns = coupling.shape[-1]
    upper_left = matmul_exact(matmul_exact(coupling, gram[..., :columns, :columns]), transpose_last(coupling))
    crosswise = matmul_exact(coupling, gram[..., :columns, columns:])
    return assemble(upper_left, crosswise, gram[..., columns:, columns:])

def lift_gram(gram, transfer):
    columns = transfer.shape[-1]
    upper_left = matmul_exact(matmul_exact(transpose_last(transfer), gram[..., :columns, :columns]), transfer)
    crosswise = matmul_exact(transpose_last(transfer), gram[..., :columns, columns:])
    return assemble(upper_left, crosswise, gram[..., columns:, columns:])

def extend_right(coefficient, transfer):
    columns = transfer.shape[-1]
    return jnp.concatenate([matmul_exact(coefficient[..., :columns], transfer), coefficient[..., columns:]], axis=-1)

def leading_space(matrix, columns):
    extent = matrix.shape[-1]
    scaling = jnp.trace(matrix, axis1=-2, axis2=-1)[..., None, None] / extent
    scaled = matrix / scaling
    current = jnp.broadcast_to(jnp.eye(extent, columns, dtype=matrix.dtype), matrix.shape[:-1] + (columns,))
    for counter in range(SWEEPS):
        current = matmul_exact(scaled, current)
        factor = jnp.linalg.cholesky(matmul_exact(transpose_last(current), current))
        current = transpose_last(jax.scipy.linalg.solve_triangular(factor, transpose_last(current), lower=True))
    return current

def reference(row_factors, col_factors, far_cols, far_coupling, row_transfer, col_transfer, par_cols, par_coupling, near_pattern, near_blocks, probes):
    rows_wide = row_factors.astype(jnp.float32)
    cols_wide = col_factors.astype(jnp.float32)
    row_gram = jnp.einsum('nri,nrj->nij', rows_wide, rows_wide, precision=HIGHEST)
    col_gram = jnp.einsum('nri,nrj->nij', cols_wide, cols_wide, precision=HIGHEST)
    probe_proj = jnp.einsum('nrk,nrp->nkp', cols_wide[..., RANK:], probes.astype(jnp.float32), precision=HIGHEST)

    def row_weight(inputs):
        chosen, coupling = inputs
        return jnp.sum(couple_block(coupling.astype(jnp.float32), col_gram[chosen]), axis=0)
    weighted = lax.map(row_weight, (far_cols, far_coupling))
    lower_factor = jnp.linalg.cholesky(row_gram)
    whitened = matmul_exact(transpose_last(lower_factor), matmul_exact(weighted, lower_factor))
    subspace = leading_space(whitened, RANK)
    coefficient = jax.scipy.linalg.solve_triangular(lower_factor, subspace, trans='T', lower=True).astype(jnp.bfloat16)
    new_basis = jnp.einsum('nri,nik->nrk', rows_wide, coefficient.astype(jnp.float32), precision=HIGHEST).astype(jnp.bfloat16)
    child_rows = extend_right(matmul_exact(transpose_last(subspace), transpose_last(lower_factor)), row_transfer.astype(jnp.float32))
    paired = child_rows.reshape(NLEAF // (2 * LEAF_DEV), 2, LEAF_DEV, RANK, EXT)
    stacked = jnp.concatenate([paired[:, 0], paired[:, 1]], axis=-2).reshape(NPAR, 2 * RANK, EXT)
    lifted = lift_gram(col_gram, col_transfer.astype(jnp.float32))
    parent_gram = lifted.reshape(NLEAF // (2 * LEAF_DEV), 2, LEAF_DEV, EXT, EXT).sum(axis=1).reshape(NPAR, EXT, EXT)

    def parent_row(inputs):
        chosen, coupling = inputs
        return jnp.sum(couple_block(coupling.astype(jnp.float32), parent_gram[chosen]), axis=0)
    parent_weight = lax.map(parent_row, (par_cols, par_coupling))
    parent_matrix = matmul_exact(matmul_exact(stacked, parent_weight), transpose_last(stacked))
    parent_transfer = leading_space(parent_matrix, RANK)

    def add_slot(index, total):
        row_id = near_pattern[index, 0]
        col_id = near_pattern[index, 1]
        weight_live = jnp.where(row_id >= 0, 1.0, 0.0).astype(jnp.float32)
        row_safe = jnp.maximum(row_id, 0).astype(jnp.int32)
        col_safe = jnp.maximum(col_id, 0).astype(jnp.int32)
        block = lax.dynamic_index_in_dim(near_blocks, index, 0, keepdims=False)
        probe_block = lax.dynamic_index_in_dim(probes, col_safe, 0, keepdims=False)
        update_rows = lax.dynamic_index_in_dim(rows_wide, row_safe, 0, keepdims=False)[:, RANK:]
        projected = lax.dynamic_index_in_dim(probe_proj, col_safe, 0, keepdims=False)
        term = jnp.dot(block.astype(jnp.float32), probe_block.astype(jnp.float32), preferred_element_type=jnp.float32) + matmul_exact(update_rows, projected)
        current = lax.dynamic_index_in_dim(total, row_safe, 0, keepdims=False)
        return lax.dynamic_update_index_in_dim(total, current + weight_live * term, row_safe, 0)
    near_image = lax.fori_loop(0, NEAR_SLOTS, add_slot, jnp.zeros((NLEAF, LEAF, PROBES), jnp.float32))
    return (new_basis, parent_transfer, near_image)
```

```python
import functools

import jax
import jax.numpy as jnp
from jax import lax
from jax.experimental import pallas as pl
from jax.experimental.pallas import tpu as pltpu
from jax.sharding import PartitionSpec as P

SWEEPS = 3
TILE = 8
F32 = jnp.float32
BF16 = jnp.bfloat16

NN = (((1,), (0,)), ((), ()))
NT = (((1,), (1,)), ((), ()))
TN = (((0,), (0,)), ((), ()))


def dot(left, right, dims=NN):
    return lax.dot_general(left, right, dims, preferred_element_type=F32)


def halves(value):
    high = value.astype(BF16)
    return high, (value - high.astype(F32)).astype(BF16)


def dot_wide(left, right, dims=NN):
    left_high, left_low = halves(left)
    right_high, right_low = halves(right)
    return (
        dot(left_high, right_high, dims)
        + dot(left_high, right_low, dims)
        + dot(left_low, right_high, dims)
    )


def dot_exact_left(left, right, dims=NN):
    high, low = halves(right)
    return dot(left, high, dims) + dot(left, low, dims)


def dot_exact_right(left, right, dims=NN):
    high, low = halves(left)
    return dot(high, right, dims) + dot(low, right, dims)


def eliminate(matrices, sides, keep=False):
    order = matrices[0].shape[0]
    count = order // TILE
    inside = lax.broadcasted_iota(jnp.int32, (TILE, 1), 0)
    tiles = [[m[r * TILE : (r + 1) * TILE] for r in range(count)] for m in matrices]
    ends = [[y[r * TILE : (r + 1) * TILE] for r in range(count)] for y in sides]
    for step in range(order):
        at, row = divmod(step, TILE)
        for tile, end in zip(tiles, ends):
            pivot = tile[at][row : row + 1]
            tail = end[at][row : row + 1]
            root = lax.rsqrt(pivot[:, step : step + 1])
            inverse = root * root
            pivot_scaled = pivot * inverse
            tail_scaled = tail * inverse
            for r in range(at, count):
                factor = tile[r][:, step : step + 1]
                if r == at:
                    factor = jnp.where(inside > row, factor, 0.0)
                tile[r] = tile[r] - factor * pivot_scaled
                end[r] = end[r] - factor * tail_scaled
            end[at] = jnp.where(inside == row, tail * root, end[at])
            if keep:
                tile[at] = jnp.where(inside == row, pivot * root, tile[at])
    done = [jnp.concatenate(end, axis=0) for end in ends]
    if not keep:
        return done
    rows = lax.broadcasted_iota(jnp.int32, (order, order), 0)
    cols = lax.broadcasted_iota(jnp.int32, (order, order), 1)
    uppers = [
        jnp.where(cols >= rows, jnp.concatenate(tile, axis=0), 0.0) for tile in tiles
    ]
    return done, uppers


def eye(order):
    rows = lax.broadcasted_iota(jnp.int32, (order, order), 0)
    cols = lax.broadcasted_iota(jnp.int32, (order, order), 1)
    return jnp.where(rows == cols, 1.0, 0.0).astype(F32)


def factor_kernel(rows_ref, upper_ref, inverse_ref):
    shards, leaves, local, extent = rows_ref.shape
    half = extent // 2
    grams = []
    for t in range(leaves):
        rows = rows_ref[:, t].reshape(shards * local, extent)
        grams.append(dot(rows, rows, TN))
    unit = eye(half)
    sides = [jnp.concatenate([g[:half, half:], unit], axis=1) for g in grams]
    firsts, upper_firsts = eliminate([g[:half, :half] for g in grams], sides, True)
    schurs = [
        g[half:, half:] - dot_wide(f[:, :half], f[:, :half], TN)
        for g, f in zip(grams, firsts)
    ]
    seconds, upper_seconds = eliminate(schurs, [unit] * leaves, True)
    for t in range(leaves):
        cross, first_inverse = firsts[t][:, :half], firsts[t][:, half:]
        upper_ref[t, :half, :half] = upper_firsts[t]
        upper_ref[t, :half, half:] = cross
        upper_ref[t, half:, :half] = jnp.zeros((half, half), F32)
        upper_ref[t, half:, half:] = upper_seconds[t]
        inverse_ref[t, :half, :half] = first_inverse
        inverse_ref[t, :half, half:] = jnp.zeros((half, half), F32)
        inverse_ref[t, half:, :half] = -dot_wide(
            seconds[t], dot_wide(cross, first_inverse, TN)
        )
        inverse_ref[t, half:, half:] = seconds[t]


def couple_sum(couplings, grams):
    half = couplings[0].shape[0]
    stacked = jnp.concatenate(couplings, axis=1)
    right = jnp.concatenate(
        [
            jnp.concatenate(
                [dot_exact_right(p[:half, :half], s, NT), p[:half, half:]], axis=1
            )
            for s, p in zip(couplings, grams)
        ],
        axis=0,
    )
    upper = dot_exact_left(stacked, right)
    lower_right = functools.reduce(jnp.add, [p[half:, half:] for p in grams])
    return upper[:, :half], upper[:, half:], lower_right


def couple_kernel(
    place_ref, far_ref, par_ref, *refs
):
    rings = refs[:8]
    far_coupling_ref, par_coupling_ref, transfer_ref = refs[8:11]
    part_ref, update_ref, gram_ref, parent_ref = refs[11:]
    columns, rank = transfer_ref.shape[0], transfer_ref.shape[1]
    leaves, far_row = far_coupling_ref.shape[0], far_coupling_ref.shape[1]
    parents, par_row = par_coupling_ref.shape[0], par_coupling_ref.shape[1]
    ring_y = rings[0].shape[0]
    local = rings[0].shape[2]
    place_z, place_y = place_ref[0], place_ref[1]
    for s in range(columns):
        slab = jnp.concatenate(
            [r[:, s].reshape(ring_y * local, 2 * rank) for r in rings], axis=0
        )
        gram_ref[s] = dot(slab, slab, TN)
    for far_z, ring in enumerate(rings):
        z = (place_z + RING_Z[far_z]) % len(rings)
        for far_y in range(ring_y):
            y = (place_y + RING_Y[far_y]) % ring_y
            at = pl.multiple_of((z * ring_y + y) * local, local)
            for s in range(columns):
                update_ref[s, pl.ds(at, local), :] = ring[far_y, s, :, rank:]
    for q in range(columns // 2):
        group, inner = divmod(q, leaves)
        child = 2 * group * leaves + inner
        total = None
        for c in (child, child + leaves):
            gram, transfer = gram_ref[c], transfer_ref[c]
            upper = dot(transfer, halves(gram[:rank])[0], TN) + dot(
                transfer, halves(gram[:rank])[1], TN
            )
            lifted = (
                dot_exact_right(upper[:, :rank], transfer),
                upper[:, rank:],
                gram[rank:, rank:],
            )
            total = lifted if total is None else tuple(a + b for a, b in zip(total, lifted))
        parent_ref[q, :rank, :rank] = total[0]
        parent_ref[q, :rank, rank:] = total[1]
        parent_ref[q, rank:, rank:] = total[2]
    jobs = [(t, far_coupling_ref, far_ref, gram_ref, t, far_row) for t in range(leaves)]
    jobs += [
        (leaves + p, par_coupling_ref, par_ref, parent_ref, p, par_row)
        for p in range(parents)
    ]
    for out, coupling_ref, cols_ref, source_ref, t, width in jobs:
        upper_left, crosswise, lower_right = couple_sum(
            [coupling_ref[t, k] for k in range(width)],
            [source_ref[cols_ref[t, k]] for k in range(width)],
        )
        part_ref[out, :rank, :rank] = upper_left
        part_ref[out, :rank, rank:] = crosswise
        part_ref[out, rank:, :rank] = crosswise.T
        part_ref[out, rank:, rank:] = lower_right


def leading(matrices, rank):
    extent = matrices[0].shape[0]
    scaled = []
    on_diagonal = eye(extent)
    for matrix in matrices:
        diagonal = jnp.sum(matrix * on_diagonal, axis=0, keepdims=True)
        trace = jnp.sum(diagonal, axis=1, keepdims=True)
        scaled.append(matrix * (extent / trace))
    current = [s[:rank] for s in scaled]
    for sweep in range(SWEEPS):
        if sweep:
            current = [dot_wide(c, s) for c, s in zip(current, scaled)]
        current = eliminate([dot_wide(c, c, NT) for c in current], current)
    return current


def leaf_kernel(weighted_ref, upper_ref, inverse_ref, rows_ref, transfer_ref, basis_ref, child_ref):
    leaves, rank = transfer_ref.shape[0], transfer_ref.shape[1]
    whitened = []
    for t in range(leaves):
        upper = upper_ref[t]
        whitened.append(dot_wide(dot_wide(upper, weighted_ref[t]), upper, NT))
    spaces = leading(whitened, rank)
    for t in range(leaves):
        space = spaces[t]
        coefficient = dot_wide(space, inverse_ref[t]).astype(BF16)
        basis_ref[t] = dot(rows_ref[t], coefficient, NT).astype(BF16)
        child = dot_wide(space, upper_ref[t])
        child_ref[t, :, :rank] = dot_exact_right(child[:, :rank], transfer_ref[t])
        child_ref[t, :, rank:] = child[:, rank:]


def parent_kernel(place_ref, own_ref, incoming_ref, weight_ref, out_ref):
    parents, rank = incoming_ref.shape[0], incoming_ref.shape[1]
    odd = place_ref[0]
    matrices = []
    for p in range(parents):
        own, incoming = own_ref[odd * parents + p], incoming_ref[p]
        first = jnp.where(odd == 0, own, incoming)
        second = jnp.where(odd == 0, incoming, own)
        stacked = jnp.concatenate([first, second], axis=0)
        matrices.append(dot_wide(dot_wide(stacked, weight_ref[p]), stacked, NT))
    for p, space in enumerate(leading(matrices, rank)):
        out_ref[p] = space.T


def near_kernel(
    row_ref, slot_ref, col_ref, block_ref, probe_ref, update_ref, rows_ref, out_ref, total_ref, proj_ref
):
    slot = pl.program_id(0)
    shards, leaves, local, extent = rows_ref.shape
    rank = extent // 2

    @pl.when(slot == 0)
    def _():
        total_ref[...] = jnp.zeros_like(total_ref)
        proj_ref[...] = jnp.zeros_like(proj_ref)

    row = row_ref[slot]

    @pl.when(row >= 0)
    def _():
        probe = probe_ref[...].reshape(shards * local, probe_ref.shape[-1])
        total_ref[row] += dot(block_ref[0], probe)
        proj_ref[row] += dot(update_ref[0], probe, TN)

    @pl.when(slot == pl.num_programs(0) - 1)
    def _():
        for t in range(leaves):
            for c in range(shards):
                updated = total_ref[t, c * local : (c + 1) * local] + dot_exact_left(
                    rows_ref[c, t, :, rank:], proj_ref[t]
                )
                out_ref[c, t] = updated.astype(BF16)


def whole(shape):
    return pl.BlockSpec(shape, lambda *_: (0,) * len(shape))


def call(body, outs, args, scalars=(), scratch=()):
    spec = pltpu.PrefetchScalarGridSpec(
        num_scalar_prefetch=len(scalars),
        grid=(1,),
        in_specs=[whole(a.shape) for a in args],
        out_specs=[whole(o.shape) for o in outs],
        scratch_shapes=list(scratch),
    )
    return pl.pallas_call(
        body,
        grid_spec=spec,
        out_shape=outs,
        compiler_params=pltpu.CompilerParams(vmem_limit_bytes=48 << 20),
    )(*scalars, *args)


LEAF_Y = 4
LEAF_Z = 8
RING_Z = (0, -1, 1, -2, 2, -3, 3, -4)
RING_Y = (0, -1, 1, 2)


def sent(value, axis, target):
    count = lax.axis_size(axis)
    return lax.ppermute(value, axis, [(d, target(d)) for d in range(count)])


def along_y(by):
    return lambda d: d // LEAF_Y * LEAF_Y + (d + by) % LEAF_Y


def along_z(by):
    return lambda d: (d + by * LEAF_Y) % (LEAF_Y * LEAF_Z)


def other_core(d):
    return d ^ 1


def along_x(by):
    return lambda d: (d + 2 * by) % 8


def gather_columns(columns):
    pieces = [
        columns,
        sent(columns, "leaf", along_y(1)),
        sent(columns, "leaf", along_y(-1)),
        sent(columns, "leaf", along_y(2)),
    ]
    start = jnp.stack(pieces)
    rings = [start]
    up = down = start
    for hop in range(LEAF_Z // 2):
        up = sent(up, "leaf", along_z(1))
        rings.append(up)
        if hop < LEAF_Z // 2 - 1:
            down = sent(down, "leaf", along_z(-1))
            rings.append(down)
    return rings


def sum_over_columns(part, core):
    half = part.shape[0] // 2
    away = lax.dynamic_slice_in_dim(part, (1 - core) * half, half, 0)
    mine = lax.dynamic_slice_in_dim(part, core * half, half, 0)
    mine = mine + sent(away, "col", other_core)
    across = [sent(mine, "col", along_x(by)) for by in (1, -1, 2)]
    total = (mine + across[2]) + (across[0] + across[1])
    other = sent(total, "col", other_core)
    return jnp.where(
        core == 0,
        jnp.concatenate([total, other], axis=0),
        jnp.concatenate([other, total], axis=0),
    )


def scatter_over_columns(parts, place, core):
    grouped = parts.reshape((4, 2) + parts.shape[1:])
    away = lax.dynamic_index_in_dim(grouped, 1 - core, 1, keepdims=False)
    mine = lax.dynamic_index_in_dim(grouped, core, 1, keepdims=False)
    paired = mine.astype(F32) + sent(away, "col", other_core).astype(F32)
    at = place // 2
    narrow = paired.astype(BF16)
    total = lax.dynamic_index_in_dim(paired, at, 0, keepdims=False)
    for by in (1, -1, 2):
        piece = lax.dynamic_index_in_dim(narrow, (at + by) % 4, 0, keepdims=False)
        total = total + sent(piece, "col", along_x(by)).astype(F32)
    return total


def on_device(
    row_factors,
    col_factors,
    far_cols,
    far_coupling,
    row_transfer,
    col_transfer,
    par_cols,
    par_coupling,
    near_pattern,
    near_blocks,
    probes,
):
    leaves, local_rows, extent = row_factors.shape
    rank = far_coupling.shape[-1]
    columns, col_rows = col_factors.shape[:2]
    probe_count = probes.shape[-1]
    parents = par_cols.shape[0]
    slots = near_blocks.shape[0]
    leaf_place = lax.axis_index("leaf")
    col_place = lax.axis_index("col")
    core = col_place % 2
    y_groups = [[z * LEAF_Y + y for y in range(LEAF_Y)] for z in range(LEAF_Z)]
    z_groups = [[z * LEAF_Y + y for z in range(LEAF_Z)] for y in range(LEAF_Y)]

    all_rows = lax.all_gather(row_factors, "col", axis=0)
    probes_y = lax.all_gather(probes, "leaf", axis=0, axis_index_groups=y_groups)
    all_probes = lax.all_gather(probes_y, "leaf", axis=0, axis_index_groups=z_groups)
    all_probes = all_probes.reshape(LEAF_Z * LEAF_Y, columns, col_rows, probe_count)

    rings = gather_columns(col_factors)
    square = jax.ShapeDtypeStruct((leaves, extent, extent), F32)
    upper, inverse = call(factor_kernel, [square, square], [all_rows])

    place = jnp.stack([leaf_place // LEAF_Y, leaf_place % LEAF_Y]).astype(jnp.int32)
    part, updates = call(
        couple_kernel,
        [
            jax.ShapeDtypeStruct((leaves + parents, extent, extent), F32),
            jax.ShapeDtypeStruct((columns, LEAF_Z * LEAF_Y * col_rows, rank), BF16),
        ],
        [*rings, far_coupling, par_coupling, col_transfer],
        [place, far_cols - col_place * columns, par_cols - col_place * (columns // 2)],
        [
            pltpu.VMEM((columns, extent, extent), F32),
            pltpu.VMEM((columns // 2, extent, extent), F32),
        ],
    )
    weights = sum_over_columns(part, core)
    weighted, parent_weight = weights[:leaves], weights[leaves:]

    new_basis, child_rows = call(
        leaf_kernel,
        [
            jax.ShapeDtypeStruct((leaves, local_rows, rank), BF16),
            jax.ShapeDtypeStruct((leaves, rank, extent), F32),
        ],
        [weighted, upper, inverse, row_factors, row_transfer],
    )
    odd = leaf_place % 2
    outgoing = lax.dynamic_slice_in_dim(child_rows, (1 - odd) * parents, parents, 0)
    incoming = sent(outgoing, "leaf", lambda d: d ^ 1)
    [parent_transfer] = call(
        parent_kernel,
        [jax.ShapeDtypeStruct((parents, extent, rank), F32)],
        [child_rows, incoming, parent_weight],
        [odd.astype(jnp.int32).reshape(1)],
    )

    live = near_pattern[:, 0] >= 0
    last = jnp.maximum(jnp.sum(live.astype(jnp.int32)) - 1, 0)
    order = jnp.minimum(jnp.arange(slots, dtype=jnp.int32), last)
    row_local = jnp.where(live, near_pattern[:, 0] - leaf_place * leaves, -1)
    col_local = jnp.where(live, near_pattern[:, 1] - col_place * columns, 0)
    picked = jnp.sum(
        jnp.where(order[:, None] == jnp.arange(slots)[None, :], col_local[None, :], 0), axis=1
    )
    row_local, picked = row_local.astype(jnp.int32), picked.astype(jnp.int32)
    shards = all_rows.shape[0]
    images = pl.pallas_call(
        near_kernel,
        grid_spec=pltpu.PrefetchScalarGridSpec(
            num_scalar_prefetch=3,
            grid=(slots,),
            in_specs=[
                pl.BlockSpec((1,) + near_blocks.shape[1:], lambda k, r, o, c: (o[k], 0, 0)),
                pl.BlockSpec(
                    (LEAF_Z * LEAF_Y, None, col_rows, probe_count), lambda k, r, o, c: (0, c[k], 0, 0)
                ),
                pl.BlockSpec((1,) + updates.shape[1:], lambda k, r, o, c: (c[k], 0, 0)),
                whole(all_rows.shape),
            ],
            out_specs=whole((shards, leaves, local_rows, probe_count)),
            scratch_shapes=[
                pltpu.VMEM((leaves, shards * local_rows, probe_count), F32),
                pltpu.VMEM((leaves, rank, probe_count), F32),
            ],
        ),
        out_shape=jax.ShapeDtypeStruct((shards, leaves, local_rows, probe_count), BF16),
        compiler_params=pltpu.CompilerParams(vmem_limit_bytes=48 << 20),
    )(row_local, order, picked, near_blocks, all_probes, updates, all_rows)
    near_image = scatter_over_columns(images, col_place, core)
    return (new_basis, parent_transfer, near_image)


def solution(mesh):
    placed = (
        P("leaf", "col", None),
        P("col", "leaf", None),
        P("leaf", "col"),
        P("leaf", "col", None, None),
        P("leaf", None, None),
        P("col", None, None),
        P("leaf", "col"),
        P("leaf", "col", None, None),
        P(("leaf", "col"), None),
        P(("leaf", "col"), None, None),
        P("col", "leaf", None),
    )
    return jax.shard_map(
        on_device,
        mesh=mesh,
        in_specs=placed,
        out_specs=(P("leaf", "col", None), P("leaf", None, None), P("leaf", "col", None)),
        check_vma=False,
    )
```

```python
import functools

import jax
import jax.numpy as jnp
from jax import lax
from jax.experimental import pallas as pl
from jax.experimental.pallas import tpu as pltpu
from jax.sharding import PartitionSpec as P

SWEEPS = 3
TILE = 8
LEAF_Y = 4
LEAF_Z = 8
COL_X = 4
PLACES_Z = (0, -1, 1, -2, 2, -3, 3, 4)
PLACES_Y = (0, 1, 2, -1)
PLACES_X = (0, -1, 1, 2)
Z, Y, X, CORE = range(4)
CHILD, COEFFICIENT, WEIGHT = range(3)
F32 = jnp.float32
BF16 = jnp.bfloat16

NN = (((1,), (0,)), ((), ()))
NT = (((1,), (1,)), ((), ()))
TN = (((0,), (0,)), ((), ()))


def dot(left, right, dims=NN):
    return lax.dot_general(left, right, dims, preferred_element_type=F32)


def halves(value):
    high = value.astype(BF16)
    return high, (value - high.astype(F32)).astype(BF16)


def dot_wide(left, right, dims=NN):
    left_high, left_low = halves(left)
    right_high, right_low = halves(right)
    return (
        dot(left_high, right_high, dims)
        + dot(left_high, right_low, dims)
        + dot(left_low, right_high, dims)
    )


def dot_exact_left(left, right, dims=NN):
    high, low = halves(right)
    return dot(left, high, dims) + dot(left, low, dims)


def dot_exact_right(left, right, dims=NN):
    high, low = halves(left)
    return dot(high, right, dims) + dot(low, right, dims)


def eliminate(systems, block=TILE):
    order = systems[0][0].shape[0]
    lanes = systems[0][0].shape[1]
    count = order // TILE
    inside = lax.broadcasted_iota(jnp.int32, (TILE, lanes), 0)

    def over_lanes(tile, lane):
        return jnp.broadcast_to(tile[:, lane : lane + 1], (TILE, lanes))

    def over_rows(tile, row):
        return jnp.broadcast_to(tile[row : row + 1], (TILE, lanes))

    work = [
        [[m[r * TILE : (r + 1) * TILE] for r in range(count)] for m in system]
        for system in systems
    ]
    span = range(block)
    for first in range(0, order, block):
        at, row = divmod(first, TILE)
        for parts in work:
            lead = parts[0]
            pivots = [over_lanes(lead[at], first + i) for i in span]
            d = [[over_rows(pivots[i], row + r) if r >= i else None for i in span] for r in span]
            roots = []
            for i in span:
                root = lax.rsqrt(d[i][i])
                roots.append(root)
                for r in range(i + 1, block):
                    d[r][i] = d[r][i] * root
                    for s in range(i + 1, r + 1):
                        d[r][s] = d[r][s] - d[r][i] * d[s][i]
            solved = []
            for part in parts:
                forward = []
                for i in span:
                    value = over_rows(part[at], row + i)
                    for m in range(i):
                        value = value - d[i][m] * forward[m]
                    forward.append(value * roots[i])
                backward = [None] * block
                for i in reversed(span):
                    value = forward[i]
                    for m in range(i + 1, block):
                        value = value - d[m][i] * backward[m]
                    backward[i] = value * roots[i]
                solved.append((forward, backward))
            for r in range(at, count):
                if r == at and row + block == TILE:
                    continue
                factors = [over_lanes(lead[r], first + i) for i in span]
                if r == at:
                    factors = [jnp.where(inside >= row + block, f, 0.0) for f in factors]
                for part, (_, backward) in zip(parts, solved):
                    for f, b in zip(factors, backward):
                        part[r] = part[r] - f * b
            for part, (forward, _) in zip(parts, solved):
                for i in span:
                    part[at] = jnp.where(inside == row + i, forward[i], part[at])
    return [[jnp.concatenate(part, axis=0) for part in parts] for parts in work]


def eye(order):
    rows = lax.broadcasted_iota(jnp.int32, (order, order), 0)
    cols = lax.broadcasted_iota(jnp.int32, (order, order), 1)
    return jnp.where(rows == cols, 1.0, 0.0).astype(F32)


def factor_kernel(place_ref, *refs):
    pieces = refs[: len(PLACES_X)]
    upper_ref, inverse_ref = refs[len(PLACES_X) :]
    leaves, extent = upper_ref.shape[0], upper_ref.shape[1]
    cores, local = pieces[0].shape[0], pieces[0].shape[2]
    half = extent // 2
    grams = []
    for t in range(leaves):
        leaf = place_ref[CORE] * leaves + t
        rows = jnp.concatenate(
            [p[:, leaf].reshape(cores * local, extent) for p in pieces], axis=0
        )
        grams.append(dot(rows, rows, TN))
    unit, blank = eye(half), jnp.zeros((half, half), F32)
    firsts = eliminate(
        [[g[:half], jnp.concatenate([unit, blank], axis=1)] for g in grams]
    )
    seconds = eliminate(
        [
            [
                jnp.concatenate(
                    [g[half:, half:] - dot_wide(f[0][:, half:], f[0][:, half:], TN), unit],
                    axis=1,
                )
            ]
            for g, f in zip(grams, firsts)
        ]
    )
    above = lax.broadcasted_iota(jnp.int32, (half, extent), 1) >= lax.broadcasted_iota(
        jnp.int32, (half, extent), 0
    )
    for t in range(leaves):
        first, first_inverse = firsts[t][0], firsts[t][1][:, :half]
        second, second_inverse = seconds[t][0][:, :half], seconds[t][0][:, half:]
        upper_ref[t, :half] = jnp.where(above, first, 0.0)
        upper_ref[t, half:, :half] = blank
        upper_ref[t, half:, half:] = jnp.where(above[:, :half], second, 0.0)
        inverse_ref[t, :half, :half] = first_inverse
        inverse_ref[t, :half, half:] = blank
        inverse_ref[t, half:, :half] = -dot_wide(
            second_inverse, dot_wide(first[:, half:], first_inverse, TN)
        )
        inverse_ref[t, half:, half:] = second_inverse


def couple_sum(couplings, grams):
    half = couplings[0].shape[0]
    stacked = jnp.concatenate(couplings, axis=1)
    right = jnp.concatenate(
        [
            jnp.concatenate(
                [dot_exact_right(p[:half, :half], s, NT), p[:half, half:]], axis=1
            )
            for s, p in zip(couplings, grams)
        ],
        axis=0,
    )
    upper = dot_exact_left(stacked, right)
    lower_right = functools.reduce(jnp.add, [p[half:, half:] for p in grams])
    return upper[:, :half], upper[:, half:], lower_right


def couple_kernel(place_ref, far_ref, par_ref, *refs):
    own_ref, left_ref, right_ref, early_ref, late_ref = refs[:5]
    far_coupling_ref, par_coupling_ref, transfer_ref = refs[5:8]
    mine_ref, away_ref, update_ref, gram_ref, parent_ref = refs[8:]
    columns, rank = transfer_ref.shape[0], transfer_ref.shape[1]
    leaves, far_row = far_coupling_ref.shape[0], far_coupling_ref.shape[1]
    parents, par_row = par_coupling_ref.shape[0], par_coupling_ref.shape[1]
    around, local = own_ref.shape[0], own_ref.shape[2]
    pieces = [own_ref, left_ref, right_ref, early_ref, late_ref]
    offsets = (0, -1, 1, 2, 2)
    starts = (0, 0, 0, 0, around // 2)
    for s in range(columns):
        slab = jnp.concatenate(
            [p[:, s].reshape(p.shape[0] * local, 2 * rank) for p in pieces], axis=0
        )
        gram_ref[s] = dot(slab, slab, TN)
    for piece, off_y, start in zip(pieces, offsets, starts):
        y = (place_ref[Y] + off_y + LEAF_Y) % LEAF_Y
        for i in range(piece.shape[0]):
            z = (place_ref[Z] + PLACES_Z[start + i] + LEAF_Z) % LEAF_Z
            at = pl.multiple_of((z * LEAF_Y + y) * local, local)
            for s in range(columns):
                update_ref[s, pl.ds(at, local), :] = piece[i, s, :, rank:]
    for q in range(columns // 2):
        group, inner = divmod(q, leaves)
        child = 2 * group * leaves + inner
        total = None
        for c in (child, child + leaves):
            gram, transfer = gram_ref[c], transfer_ref[c]
            upper = dot_exact_left(transfer, gram[:rank], TN)
            lifted = (
                dot_exact_right(upper[:, :rank], transfer),
                upper[:, rank:],
                gram[rank:, rank:],
            )
            total = lifted if total is None else tuple(a + b for a, b in zip(total, lifted))
        parent_ref[q, :rank, :rank] = total[0]
        parent_ref[q, :rank, rank:] = total[1]
        parent_ref[q, rank:, rank:] = total[2]
    core = place_ref[CORE]
    each = leaves // 2
    for out_ref, side in ((mine_ref, core), (away_ref, 1 - core)):
        jobs = [
            (t, far_coupling_ref, far_ref, gram_ref, side * each + t, far_row)
            for t in range(each)
        ]
        jobs.append((each, par_coupling_ref, par_ref, parent_ref, side, par_row))
        for out, coupling_ref, cols_ref, source_ref, t, width in jobs:
            upper_left, crosswise, lower_right = couple_sum(
                [coupling_ref[t, k] for k in range(width)],
                [source_ref[cols_ref[t, k]] for k in range(width)],
            )
            out_ref[out, :rank, :rank] = upper_left
            out_ref[out, :rank, rank:] = crosswise
            out_ref[out, rank:, :rank] = crosswise.T
            out_ref[out, rank:, rank:] = lower_right


def leading(matrices, rank):
    extent = matrices[0].shape[0]
    scaled = []
    on_diagonal = eye(extent)
    for matrix in matrices:
        diagonal = jnp.sum(matrix * on_diagonal, axis=0, keepdims=True)
        trace = jnp.sum(diagonal, axis=1, keepdims=True)
        scaled.append(matrix * (extent / trace))
    current = [s[:rank] for s in scaled]
    for sweep in range(SWEEPS):
        if sweep:
            current = [dot_wide(c, s) for c, s in zip(current, scaled)]
        blank = jnp.zeros((rank, extent - rank), F32)
        systems = [
            [jnp.concatenate([dot_wide(c, c, NT), blank], axis=1), c] for c in current
        ]
        current = [parts[1] for parts in eliminate(systems)]
    return current


def leaf_kernel(
    place_ref, mine_ref, left_ref, right_ref, across_ref, upper_ref, inverse_ref, transfer_ref, out_ref
):
    leaves, extent = upper_ref.shape[0], upper_ref.shape[1]
    rank = transfer_ref.shape[1]

    def summed(at):
        near = mine_ref[at].astype(F32) + across_ref[at].astype(F32)
        return near + (left_ref[at].astype(F32) + right_ref[at].astype(F32))

    whitened = []
    for t in range(leaves):
        upper = upper_ref[t]
        whitened.append(dot_wide(dot_wide(upper, summed(t)), upper, NT))
    spaces = leading(whitened, rank)
    for t in range(leaves):
        space = spaces[t]
        child = dot_wide(space, upper_ref[t])
        transfer = transfer_ref[place_ref[CORE] * leaves + t]
        rows = pl.ds(t * rank, rank)
        out_ref[CHILD, rows, :rank] = dot_exact_right(child[:, :rank], transfer)
        out_ref[CHILD, rows, rank:] = child[:, rank:]
        out_ref[COEFFICIENT, rows, :] = dot_wide(space, inverse_ref[t])
    out_ref[WEIGHT] = summed(leaves)


def parent_kernel(
    place_ref, own_ref, other_ref, same_ref, cross_ref, rows_ref, out_ref, basis_ref
):
    parents, extent, rank = out_ref.shape
    core, odd = place_ref[CORE], place_ref[Y] % 2
    kept = jnp.where(core == odd, own_ref[CHILD], other_ref[CHILD])
    incoming = jnp.where(core == odd, same_ref[...], cross_ref[...])
    first = jnp.where(odd == 0, kept, incoming)
    second = jnp.where(odd == 0, incoming, kept)
    matrices = []
    for p in range(parents):
        rows = slice(p * rank, (p + 1) * rank)
        stacked = jnp.concatenate([first[rows], second[rows]], axis=0)
        weight = jnp.where(core == p, own_ref[WEIGHT], other_ref[WEIGHT])
        matrices.append(dot_wide(dot_wide(stacked, weight), stacked, NT))
    for p, space in enumerate(leading(matrices, rank)):
        out_ref[p] = space.T
    for ref, side in ((own_ref, core), (other_ref, 1 - core)):
        for t in range(parents):
            coefficient = ref[COEFFICIENT, t * rank : (t + 1) * rank].astype(BF16)
            leaf = side * parents + t
            basis_ref[leaf] = dot(rows_ref[leaf], coefficient, NT).astype(BF16)


def near_kernel(place_ref, row_ref, col_ref, count_ref, blocks_ref, *refs):
    probes_from, update_ref, pieces, out_ref = refs[0], refs[1], refs[2:6], refs[6]
    total_ref, proj_ref, block_ref, probe_ref, block_semaphores, semaphore = refs[7:]
    slots = block_ref.shape[0]
    cores, leaves, local, extent = pieces[0].shape
    rank = extent // 2
    live = count_ref[0]
    def block_copy(k):
        return pltpu.make_async_copy(
            blocks_ref.at[k], block_ref.at[k], block_semaphores.at[k]
        )

    probe_copy = pltpu.make_async_copy(probes_from, probe_ref, semaphore.at[0])
    probe_copy.start()
    for k in range(slots):
        @pl.when(k < live)
        def _():
            block_copy(k).start()
    total_ref[...] = jnp.zeros_like(total_ref)
    proj_ref[...] = jnp.zeros_like(proj_ref)
    probe_copy.wait()

    def slot(k, carry):
        block_copy(k).wait()
        row, col = row_ref[k], col_ref[k]
        probe = jnp.concatenate(
            [
                probe_ref[z, (y - place_ref[Y] + LEAF_Y) % LEAF_Y, col]
                for z in range(LEAF_Z)
                for y in range(LEAF_Y)
            ],
            axis=0,
        )
        total_ref[row] += dot(block_ref[k], probe)
        proj_ref[row] += dot(update_ref[col], probe, TN)
        return carry

    lax.fori_loop(0, live, slot, 0)
    for i, piece in enumerate(pieces):
        x = (place_ref[X] + PLACES_X[i] + COL_X) % COL_X
        for flip in range(cores):
            core = (place_ref[CORE] + flip) % 2
            at = pl.multiple_of((x * 2 + core) * local, local)
            for t in range(leaves):
                updated = total_ref[t, pl.ds(at, local), :] + dot_exact_left(
                    piece[flip, t, :, rank:], proj_ref[t]
                )
                out_ref[core, x, t] = updated.astype(BF16)


def whole(shape):
    return pl.BlockSpec(shape, lambda *_: (0,) * len(shape))


def in_hbm(array):
    return pltpu.with_memory_space_constraint(array, pltpu.HBM)


def in_vmem(array):
    return pltpu.with_memory_space_constraint(array, pltpu.VMEM)


def call(body, outs, near, far=(), scalars=(), scratch=(), room=8):
    before, held, inner = len(scalars), len(near), len(far)
    last = before + held + inner + len(outs) + len(scratch)

    def fetched(*refs):
        named, sources = refs[: before + held], refs[before + held : before + held + inner]
        made, targets = refs[before + held + inner : last], refs[last : last + inner]
        copies = [
            pltpu.make_async_copy(source, target, refs[-1].at[i])
            for i, (source, target) in enumerate(zip(sources, targets))
        ]
        for copy in copies:
            copy.start()
        for copy in copies:
            copy.wait()
        body(*named, *targets, *made)

    return pl.pallas_call(
        fetched if inner else body,
        grid_spec=pltpu.PrefetchScalarGridSpec(
            num_scalar_prefetch=before,
            grid=(1,),
            in_specs=[pl.BlockSpec(memory_space=pltpu.VMEM) for _ in near]
            + [pl.BlockSpec(memory_space=pltpu.HBM) for _ in far],
            out_specs=[whole(o.shape) for o in outs],
            scratch_shapes=[
                *scratch,
                *[pltpu.VMEM(a.shape, a.dtype) for a in far],
                *([pltpu.SemaphoreType.DMA((inner,))] if inner else []),
            ],
        ),
        out_shape=outs,
        compiler_params=pltpu.CompilerParams(vmem_limit_bytes=room << 20),
        name=body.__name__,
    )(*scalars, *[in_vmem(a) for a in near], *[in_hbm(a) for a in far])


def sent(value, axis, target):
    count = lax.axis_size(axis)
    return lax.ppermute(value, axis, [(d, target(d)) for d in range(count)])


def along_y(by):
    return lambda d: d // LEAF_Y * LEAF_Y + (d + by) % LEAF_Y


def along_z(by):
    return lambda d: (d + by * LEAF_Y) % (LEAF_Y * LEAF_Z)


def along_x(by):
    return lambda d: (d + 2 * by) % (2 * COL_X)


def flipped(d):
    return d ^ 1


def gather_all(columns, probes, rows, place):
    start = jnp.stack([probes] + [sent(probes, "leaf", along_y(-y)) for y in PLACES_Y[1:]])
    groups = [[z * LEAF_Y + y for z in range(LEAF_Z)] for y in range(LEAF_Y)]
    all_probes = lax.all_gather(start, "leaf", axis=0, axis_index_groups=groups)
    columns, _ = lax.optimization_barrier((columns, start))
    own = jnp.stack([columns] + [sent(columns, "leaf", along_z(-z)) for z in PLACES_Z[1:]])
    pair = jnp.stack([rows, sent(rows, "col", flipped)])
    own, pair = lax.optimization_barrier((own, pair))
    left = sent(own, "leaf", along_y(1))
    right = sent(own, "leaf", along_y(-1))
    all_rows = [pair] + [sent(pair, "col", along_x(-x)) for x in PLACES_X[1:]]
    left, right, *all_rows = lax.optimization_barrier((left, right, *all_rows))
    half = own.shape[0] // 2
    early = sent(left[:half], "leaf", along_y(1))
    late = sent(right[half:], "leaf", along_y(-1))
    leaves, extent = rows.shape[0], rows.shape[2]
    square = jax.ShapeDtypeStruct((leaves // 2, extent, extent), F32)
    factors = call(factor_kernel, [square, square], all_rows, (), [place])
    own, left, right, early, late, *factors = lax.optimization_barrier(
        (own, left, right, early, late, *factors)
    )
    return (own, left, right, early, late), all_probes, all_rows, factors


def scatter_start(parts, place, core):
    away = lax.dynamic_index_in_dim(parts, 1 - core, 0, keepdims=False)
    mine = lax.dynamic_index_in_dim(parts, core, 0, keepdims=False)
    paired = mine.astype(F32) + sent(away, "col", flipped).astype(F32)
    narrow = paired.astype(BF16)
    own = lax.dynamic_index_in_dim(paired, place, 0, keepdims=False)
    pieces = [
        lax.dynamic_index_in_dim(narrow, (place + by) % COL_X, 0, keepdims=False)
        for by in (1, -1, 2)
    ]
    return pieces, own


def on_device(
    row_factors,
    col_factors,
    far_cols,
    far_coupling,
    row_transfer,
    col_transfer,
    par_cols,
    par_coupling,
    near_pattern,
    near_blocks,
    probes,
):
    leaves, local_rows, extent = row_factors.shape
    rank = far_coupling.shape[-1]
    columns, col_rows = col_factors.shape[:2]
    probe_count = probes.shape[-1]
    parents = par_cols.shape[0]
    slots = near_blocks.shape[0]
    leaf_place = lax.axis_index("leaf")
    col_place = lax.axis_index("col")
    core = col_place % 2
    place = jnp.stack(
        [leaf_place // LEAF_Y, leaf_place % LEAF_Y, col_place // 2, core]
    ).astype(jnp.int32)

    all_columns, all_probes, all_rows, (upper, inverse) = gather_all(
        col_factors, probes, row_factors, place
    )
    triple = jax.ShapeDtypeStruct((3, extent, extent), F32)
    mine, away, updates = call(
        couple_kernel,
        [
            triple,
            triple,
            jax.ShapeDtypeStruct((columns, LEAF_Z * LEAF_Y * col_rows, rank), BF16),
        ],
        all_columns,
        [far_coupling, par_coupling, col_transfer],
        [place, far_cols - col_place * columns, par_cols - col_place * (columns // 2)],
        [
            pltpu.VMEM((columns, extent, extent), F32),
            pltpu.VMEM((columns // 2, extent, extent), F32),
        ],
        14,
    )
    mine = (mine + sent(away, "col", flipped)).astype(BF16)
    across = [sent(mine, "col", along_x(by)) for by in (1, -1, 2)]
    [bundle] = call(
        leaf_kernel, [triple], [mine, *across, upper, inverse], [row_transfer], [place]
    )
    other = sent(bundle, "col", flipped)
    children = bundle[CHILD]
    same = sent(children, "leaf", flipped)
    width = 2 * COL_X
    cross = lax.ppermute(
        children,
        ("leaf", "col"),
        [(d, d // width % 2 * -width + (d // width + 1) % 2 * width + (d ^ 1)) for d in range(LEAF_Y * LEAF_Z * width)],
    )
    used = near_pattern[:, 0] >= 0
    row_local = jnp.where(used, near_pattern[:, 0] - leaf_place * leaves, 0)
    col_local = jnp.where(used, near_pattern[:, 1] - col_place * columns, 0)
    count = jnp.sum(used.astype(jnp.int32)).reshape(1)
    row_local, col_local, count, _ = lax.optimization_barrier(
        (row_local.astype(jnp.int32), col_local.astype(jnp.int32), count, bundle)
    )
    images = pl.pallas_call(
        near_kernel,
        grid_spec=pltpu.PrefetchScalarGridSpec(
            num_scalar_prefetch=4,
            grid=(1,),
            in_specs=[pl.BlockSpec(memory_space=pltpu.HBM) for _ in range(2)]
            + [pl.BlockSpec(memory_space=pltpu.VMEM) for _ in range(1 + len(all_rows))],
            out_specs=whole((2, COL_X, leaves, local_rows, probe_count)),
            scratch_shapes=[
                pltpu.VMEM((leaves, 2 * COL_X * local_rows, probe_count), F32),
                pltpu.VMEM((leaves, rank, probe_count), F32),
                pltpu.VMEM(near_blocks.shape, BF16),
                pltpu.VMEM(all_probes.shape, BF16),
                pltpu.SemaphoreType.DMA((slots,)),
                pltpu.SemaphoreType.DMA((1,)),
            ],
        ),
        out_shape=jax.ShapeDtypeStruct((2, COL_X, leaves, local_rows, probe_count), BF16),
        compiler_params=pltpu.CompilerParams(vmem_limit_bytes=26 << 20),
        name="near_kernel",
    )(
        place,
        row_local,
        col_local,
        count,
        in_hbm(near_blocks),
        in_hbm(all_probes),
        in_vmem(updates),
        *[in_vmem(piece) for piece in all_rows],
    )
    near_sent, near_own = scatter_start(images, col_place // 2, core)
    other, same, cross, *near_sent = lax.optimization_barrier((other, same, cross, *near_sent))
    near_image = near_own
    for by, piece in zip((1, -1, 2), near_sent):
        near_image = near_image + sent(piece, "col", along_x(by)).astype(F32)
    parent_transfer, new_basis = call(
        parent_kernel,
        [
            jax.ShapeDtypeStruct((parents, extent, rank), F32),
            jax.ShapeDtypeStruct((leaves, local_rows, rank), BF16),
        ],
        [bundle, other, same, cross],
        [row_factors],
        [place],
    )

    return (new_basis, parent_transfer, near_image)


def solution(mesh):
    placed = (
        P("leaf", "col", None),
        P("col", "leaf", None),
        P("leaf", "col"),
        P("leaf", "col", None, None),
        P("leaf", None, None),
        P("col", None, None),
        P("leaf", "col"),
        P("leaf", "col", None, None),
        P(("leaf", "col"), None),
        P(("leaf", "col"), None, None),
        P("col", "leaf", None),
    )
    return jax.shard_map(
        on_device,
        mesh=mesh,
        in_specs=placed,
        out_specs=(P("leaf", "col", None), P("leaf", None, None), P("leaf", "col", None)),
        check_vma=False,
    )
```

```python
import functools

import jax
import jax.numpy as jnp
from jax import lax
from jax.experimental import pallas as pl
from jax.experimental.pallas import tpu as pltpu
from jax.sharding import PartitionSpec as P

SWEEPS = 3
TILE = 8
LEAF_Y = 4
LEAF_Z = 8
COL_X = 4
PLACES_Z = (0, -1, 1, -2, 2, -3, 3, 4)
PLACES_Y = (0, 1, 2, -1)
PLACES_X = (0, -1, 1, 2)
Z, Y, X, CORE = range(4)
CHILD, COEFFICIENT, WEIGHT = range(3)
F32 = jnp.float32
BF16 = jnp.bfloat16

NN = (((1,), (0,)), ((), ()))
NT = (((1,), (1,)), ((), ()))
TN = (((0,), (0,)), ((), ()))


def dot(left, right, dims=NN):
    return lax.dot_general(left, right, dims, preferred_element_type=F32)


def halves(value):
    high = value.astype(BF16)
    return high, (value - high.astype(F32)).astype(BF16)


def dot_wide(left, right, dims=NN):
    left_high, left_low = halves(left)
    right_high, right_low = halves(right)
    return (
        dot(left_high, right_high, dims)
        + dot(left_high, right_low, dims)
        + dot(left_low, right_high, dims)
    )


def dot_exact_left(left, right, dims=NN):
    high, low = halves(right)
    return dot(left, high, dims) + dot(left, low, dims)


def dot_exact_right(left, right, dims=NN):
    high, low = halves(left)
    return dot(high, right, dims) + dot(low, right, dims)


def eliminate(systems, block=TILE):
    order = systems[0][0].shape[0]
    lanes = systems[0][0].shape[1]
    count = order // TILE
    inside = lax.broadcasted_iota(jnp.int32, (TILE, lanes), 0)

    def over_lanes(tile, lane):
        return jnp.broadcast_to(tile[:, lane : lane + 1], (TILE, lanes))

    def over_rows(tile, row):
        return jnp.broadcast_to(tile[row : row + 1], (TILE, lanes))

    work = [
        [[m[r * TILE : (r + 1) * TILE] for r in range(count)] for m in system]
        for system in systems
    ]
    span = range(block)
    for first in range(0, order, block):
        at, row = divmod(first, TILE)
        for parts in work:
            lead = parts[0]
            pivots = [over_lanes(lead[at], first + i) for i in span]
            d = [[over_rows(pivots[i], row + r) if r >= i else None for i in span] for r in span]
            roots = []
            for i in span:
                root = lax.rsqrt(d[i][i])
                roots.append(root)
                for r in range(i + 1, block):
                    d[r][i] = d[r][i] * root
                    for s in range(i + 1, r + 1):
                        d[r][s] = d[r][s] - d[r][i] * d[s][i]
            solved = []
            for part in parts:
                forward = []
                for i in span:
                    value = over_rows(part[at], row + i)
                    for m in range(i):
                        value = value - d[i][m] * forward[m]
                    forward.append(value * roots[i])
                backward = [None] * block
                for i in reversed(span):
                    value = forward[i]
                    for m in range(i + 1, block):
                        value = value - d[m][i] * backward[m]
                    backward[i] = value * roots[i]
                solved.append((forward, backward))
            for r in range(at, count):
                if r == at and row + block == TILE:
                    continue
                factors = [over_lanes(lead[r], first + i) for i in span]
                if r == at:
                    factors = [jnp.where(inside >= row + block, f, 0.0) for f in factors]
                for part, (_, backward) in zip(parts, solved):
                    for f, b in zip(factors, backward):
                        part[r] = part[r] - f * b
            for part, (forward, _) in zip(parts, solved):
                for i in span:
                    part[at] = jnp.where(inside == row + i, forward[i], part[at])
    return [[jnp.concatenate(part, axis=0) for part in parts] for parts in work]


def eye(order):
    rows = lax.broadcasted_iota(jnp.int32, (order, order), 0)
    cols = lax.broadcasted_iota(jnp.int32, (order, order), 1)
    return jnp.where(rows == cols, 1.0, 0.0).astype(F32)


def factor_kernel(place_ref, *refs):
    pieces = refs[: len(PLACES_X)]
    upper_ref, inverse_ref = refs[len(PLACES_X) :]
    leaves, extent = upper_ref.shape[0], upper_ref.shape[1]
    cores, local = pieces[0].shape[0], pieces[0].shape[2]
    half = extent // 2
    grams = []
    for t in range(leaves):
        leaf = place_ref[CORE] * leaves + t
        rows = jnp.concatenate(
            [p[:, leaf].reshape(cores * local, extent) for p in pieces], axis=0
        )
        grams.append(dot(rows, rows, TN))
    unit, blank = eye(half), jnp.zeros((half, half), F32)
    firsts = eliminate(
        [[g[:half], jnp.concatenate([unit, blank], axis=1)] for g in grams]
    )
    seconds = eliminate(
        [
            [
                jnp.concatenate(
                    [g[half:, half:] - dot_wide(f[0][:, half:], f[0][:, half:], TN), unit],
                    axis=1,
                )
            ]
            for g, f in zip(grams, firsts)
        ]
    )
    above = lax.broadcasted_iota(jnp.int32, (half, extent), 1) >= lax.broadcasted_iota(
        jnp.int32, (half, extent), 0
    )
    for t in range(leaves):
        first, first_inverse = firsts[t][0], firsts[t][1][:, :half]
        second, second_inverse = seconds[t][0][:, :half], seconds[t][0][:, half:]
        upper_ref[t, :half] = jnp.where(above, first, 0.0)
        upper_ref[t, half:, :half] = blank
        upper_ref[t, half:, half:] = jnp.where(above[:, :half], second, 0.0)
        inverse_ref[t, :half, :half] = first_inverse
        inverse_ref[t, :half, half:] = blank
        inverse_ref[t, half:, :half] = -dot_wide(
            second_inverse, dot_wide(first[:, half:], first_inverse, TN)
        )
        inverse_ref[t, half:, half:] = second_inverse


def couple_sum(couplings, grams):
    half = couplings[0].shape[0]
    stacked = jnp.concatenate(couplings, axis=1)
    right = jnp.concatenate(
        [
            jnp.concatenate(
                [dot_exact_right(p[:half, :half], s, NT), p[:half, half:]], axis=1
            )
            for s, p in zip(couplings, grams)
        ],
        axis=0,
    )
    upper = dot_exact_left(stacked, right)
    lower_right = functools.reduce(jnp.add, [p[half:, half:] for p in grams])
    return upper[:, :half], upper[:, half:], lower_right


def couple_kernel(place_ref, far_ref, par_ref, *refs):
    own_ref, left_ref, right_ref, early_ref, late_ref = refs[:5]
    far_coupling_ref, par_coupling_ref, transfer_ref = refs[5:8]
    mine_ref, away_ref, update_ref, gram_ref, parent_ref = refs[8:]
    columns, rank = transfer_ref.shape[0], transfer_ref.shape[1]
    leaves, far_row = far_coupling_ref.shape[0], far_coupling_ref.shape[1]
    parents, par_row = par_coupling_ref.shape[0], par_coupling_ref.shape[1]
    around, local = own_ref.shape[0], own_ref.shape[2]
    pieces = [own_ref, left_ref, right_ref, early_ref, late_ref]
    offsets = (0, -1, 1, 2, 2)
    starts = (0, 0, 0, 0, around // 2)
    for s in range(columns):
        slab = jnp.concatenate(
            [p[:, s].reshape(p.shape[0] * local, 2 * rank) for p in pieces], axis=0
        )
        gram_ref[s] = dot(slab, slab, TN)
    for piece, off_y, start in zip(pieces, offsets, starts):
        y = (place_ref[Y] + off_y + LEAF_Y) % LEAF_Y
        for i in range(piece.shape[0]):
            z = (place_ref[Z] + PLACES_Z[start + i] + LEAF_Z) % LEAF_Z
            at = pl.multiple_of((z * LEAF_Y + y) * local, local)
            for s in range(columns):
                update_ref[s, pl.ds(at, local), :] = piece[i, s, :, rank:]
    for q in range(columns // 2):
        group, inner = divmod(q, leaves)
        child = 2 * group * leaves + inner
        total = None
        for c in (child, child + leaves):
            gram, transfer = gram_ref[c], transfer_ref[c]
            upper = dot_exact_left(transfer, gram[:rank], TN)
            lifted = (
                dot_exact_right(upper[:, :rank], transfer),
                upper[:, rank:],
                gram[rank:, rank:],
            )
            total = lifted if total is None else tuple(a + b for a, b in zip(total, lifted))
        parent_ref[q, :rank, :rank] = total[0]
        parent_ref[q, :rank, rank:] = total[1]
        parent_ref[q, rank:, rank:] = total[2]
    core = place_ref[CORE]
    each = leaves // 2
    for out_ref, side in ((mine_ref, core), (away_ref, 1 - core)):
        jobs = [
            (t, far_coupling_ref, far_ref, gram_ref, side * each + t, far_row)
            for t in range(each)
        ]
        jobs.append((each, par_coupling_ref, par_ref, parent_ref, side, par_row))
        for out, coupling_ref, cols_ref, source_ref, t, width in jobs:
            upper_left, crosswise, lower_right = couple_sum(
                [coupling_ref[t, k] for k in range(width)],
                [source_ref[cols_ref[t, k]] for k in range(width)],
            )
            out_ref[out, :rank, :rank] = upper_left
            out_ref[out, :rank, rank:] = crosswise
            out_ref[out, rank:, :rank] = crosswise.T
            out_ref[out, rank:, rank:] = lower_right


def leading(matrices, rank):
    extent = matrices[0].shape[0]
    scaled = []
    on_diagonal = eye(extent)
    for matrix in matrices:
        diagonal = jnp.sum(matrix * on_diagonal, axis=0, keepdims=True)
        trace = jnp.sum(diagonal, axis=1, keepdims=True)
        scaled.append(matrix * (extent / trace))
    current = [s[:rank] for s in scaled]
    for sweep in range(SWEEPS):
        if sweep:
            current = [dot_wide(c, s) for c, s in zip(current, scaled)]
        blank = jnp.zeros((rank, extent - rank), F32)
        systems = [
            [jnp.concatenate([dot_wide(c, c, NT), blank], axis=1), c] for c in current
        ]
        current = [parts[1] for parts in eliminate(systems)]
    return current


def leaf_kernel(
    place_ref, mine_ref, left_ref, right_ref, across_ref, upper_ref, inverse_ref, transfer_ref, out_ref
):
    leaves, extent = upper_ref.shape[0], upper_ref.shape[1]
    rank = transfer_ref.shape[1]

    def summed(at):
        near = mine_ref[at].astype(F32) + across_ref[at].astype(F32)
        return near + (left_ref[at].astype(F32) + right_ref[at].astype(F32))

    whitened = []
    for t in range(leaves):
        upper = upper_ref[t]
        whitened.append(dot_wide(dot_wide(upper, summed(t)), upper, NT))
    spaces = leading(whitened, rank)
    for t in range(leaves):
        space = spaces[t]
        child = dot_wide(space, upper_ref[t])
        transfer = transfer_ref[place_ref[CORE] * leaves + t]
        rows = pl.ds(t * rank, rank)
        out_ref[CHILD, rows, :rank] = dot_exact_right(child[:, :rank], transfer)
        out_ref[CHILD, rows, rank:] = child[:, rank:]
        out_ref[COEFFICIENT, rows, :] = dot_wide(space, inverse_ref[t])
    out_ref[WEIGHT] = summed(leaves)


def parent_kernel(
    place_ref, own_ref, other_ref, same_ref, cross_ref, rows_ref, out_ref, basis_ref
):
    parents, rank, extent = out_ref.shape
    core, odd = place_ref[CORE], place_ref[Y] % 2
    kept = jnp.where(core == odd, own_ref[CHILD], other_ref[CHILD])
    incoming = jnp.where(core == odd, same_ref[...], cross_ref[...])
    first = jnp.where(odd == 0, kept, incoming)
    second = jnp.where(odd == 0, incoming, kept)
    matrices = []
    for p in range(parents):
        rows = slice(p * rank, (p + 1) * rank)
        stacked = jnp.concatenate([first[rows], second[rows]], axis=0)
        weight = jnp.where(core == p, own_ref[WEIGHT], other_ref[WEIGHT])
        matrices.append(dot_wide(dot_wide(stacked, weight), stacked, NT))
    for p, space in enumerate(leading(matrices, rank)):
        out_ref[p] = space
    for ref, side in ((own_ref, core), (other_ref, 1 - core)):
        for t in range(parents):
            coefficient = ref[COEFFICIENT, t * rank : (t + 1) * rank].astype(BF16)
            leaf = side * parents + t
            basis_ref[leaf] = dot(rows_ref[leaf], coefficient, NT).astype(BF16)


def near_kernel(place_ref, row_ref, col_ref, count_ref, blocks_ref, *refs):
    probes_from, update_ref, pieces_from, out_ref = refs[0], refs[1], refs[2:6], refs[6]
    total_ref, proj_ref, block_ref, probe_ref, pieces_ref = refs[7:12]
    block_semaphores, semaphores = refs[12:]
    slots = block_ref.shape[0]
    cores, leaves, local, extent = pieces_from[0].shape
    rank = extent // 2
    live = count_ref[0]
    def block_copy(k):
        return pltpu.make_async_copy(
            blocks_ref.at[k], block_ref.at[k], block_semaphores.at[k]
        )

    copies = [pltpu.make_async_copy(probes_from, probe_ref, semaphores.at[0])]
    for i, piece in enumerate(pieces_from):
        copies.append(pltpu.make_async_copy(piece, pieces_ref.at[i], semaphores.at[i + 1]))
    for copy in copies:
        copy.start()
    for k in range(slots):
        @pl.when(k < live)
        def _():
            block_copy(k).start()
    total_ref[...] = jnp.zeros_like(total_ref)
    proj_ref[...] = jnp.zeros_like(proj_ref)
    for copy in copies:
        copy.wait()

    def slot(k, carry):
        block_copy(k).wait()
        row, col = row_ref[k], col_ref[k]
        probe = jnp.concatenate(
            [
                probe_ref[z, (y - place_ref[Y] + LEAF_Y) % LEAF_Y, col]
                for z in range(LEAF_Z)
                for y in range(LEAF_Y)
            ],
            axis=0,
        )
        total_ref[row] += dot(block_ref[k], probe)
        proj_ref[row] += dot(update_ref[col], probe, TN)
        return carry

    lax.fori_loop(0, live, slot, 0)
    for i in range(len(pieces_from)):
        x = (place_ref[X] + PLACES_X[i] + COL_X) % COL_X
        for flip in range(cores):
            core = (place_ref[CORE] + flip) % 2
            at = pl.multiple_of((x * 2 + core) * local, local)
            for t in range(leaves):
                updated = total_ref[t, pl.ds(at, local), :] + dot_exact_left(
                    pieces_ref[i, flip, t, :, rank:], proj_ref[t]
                )
                out_ref[core, x, t] = updated.astype(BF16)


def whole(shape):
    return pl.BlockSpec(shape, lambda *_: (0,) * len(shape))


def in_hbm(array):
    return pltpu.with_memory_space_constraint(array, pltpu.HBM)


def in_vmem(array):
    return pltpu.with_memory_space_constraint(array, pltpu.VMEM)


def call(body, outs, near, far=(), scalars=(), scratch=(), room=8):
    before, held, inner = len(scalars), len(near), len(far)
    last = before + held + inner + len(outs) + len(scratch)

    def fetched(*refs):
        named, sources = refs[: before + held], refs[before + held : before + held + inner]
        made, targets = refs[before + held + inner : last], refs[last : last + inner]
        copies = [
            pltpu.make_async_copy(source, target, refs[-1].at[i])
            for i, (source, target) in enumerate(zip(sources, targets))
        ]
        for copy in copies:
            copy.start()
        for copy in copies:
            copy.wait()
        body(*named, *targets, *made)

    return pl.pallas_call(
        fetched if inner else body,
        grid_spec=pltpu.PrefetchScalarGridSpec(
            num_scalar_prefetch=before,
            grid=(1,),
            in_specs=[pl.BlockSpec(memory_space=pltpu.VMEM) for _ in near]
            + [pl.BlockSpec(memory_space=pltpu.HBM) for _ in far],
            out_specs=[whole(o.shape) for o in outs],
            scratch_shapes=[
                *scratch,
                *[pltpu.VMEM(a.shape, a.dtype) for a in far],
                *([pltpu.SemaphoreType.DMA((inner,))] if inner else []),
            ],
        ),
        out_shape=outs,
        compiler_params=pltpu.CompilerParams(vmem_limit_bytes=room << 20),
        name=body.__name__,
    )(*scalars, *[in_vmem(a) for a in near], *[in_hbm(a) for a in far])


def sent(value, axis, target):
    count = lax.axis_size(axis)
    return lax.ppermute(value, axis, [(d, target(d)) for d in range(count)])


def along_y(by):
    return lambda d: d // LEAF_Y * LEAF_Y + (d + by) % LEAF_Y


def along_z(by):
    return lambda d: (d + by * LEAF_Y) % (LEAF_Y * LEAF_Z)


def along_x(by):
    return lambda d: (d + 2 * by) % (2 * COL_X)


def flipped(d):
    return d ^ 1


def gather_all(columns, probes, rows, place):
    start = jnp.stack([probes] + [sent(probes, "leaf", along_y(-y)) for y in PLACES_Y[1:]])
    groups = [[z * LEAF_Y + y for z in range(LEAF_Z)] for y in range(LEAF_Y)]
    all_probes = lax.all_gather(start, "leaf", axis=0, axis_index_groups=groups)
    columns, _ = lax.optimization_barrier((columns, start))
    own = jnp.stack([columns] + [sent(columns, "leaf", along_z(-z)) for z in PLACES_Z[1:]])
    pair = jnp.stack([rows, sent(rows, "col", flipped)])
    own, pair = lax.optimization_barrier((own, pair))
    left = sent(own, "leaf", along_y(1))
    right = sent(own, "leaf", along_y(-1))
    all_rows = [pair] + [sent(pair, "col", along_x(-x)) for x in PLACES_X[1:]]
    left, right, *all_rows = lax.optimization_barrier((left, right, *all_rows))
    half = own.shape[0] // 2
    early = sent(left[:half], "leaf", along_y(1))
    late = sent(right[half:], "leaf", along_y(-1))
    leaves, extent = rows.shape[0], rows.shape[2]
    square = jax.ShapeDtypeStruct((leaves // 2, extent, extent), F32)
    factors = call(factor_kernel, [square, square], all_rows, (), [place])
    own, left, right, early, late, *factors = lax.optimization_barrier(
        (own, left, right, early, late, *factors)
    )
    return (own, left, right, early, late), all_probes, all_rows, factors


def scatter_start(parts, place, core):
    away = lax.dynamic_index_in_dim(parts, 1 - core, 0, keepdims=False)
    mine = lax.dynamic_index_in_dim(parts, core, 0, keepdims=False)
    paired = mine.astype(F32) + sent(away, "col", flipped).astype(F32)
    narrow = paired.astype(BF16)
    own = lax.dynamic_index_in_dim(paired, place, 0, keepdims=False)
    pieces = [
        lax.dynamic_index_in_dim(narrow, (place + by) % COL_X, 0, keepdims=False)
        for by in (1, -1, 2)
    ]
    return pieces, own


def on_device(
    row_factors,
    col_factors,
    far_cols,
    far_coupling,
    row_transfer,
    col_transfer,
    par_cols,
    par_coupling,
    near_pattern,
    near_blocks,
    probes,
):
    leaves, local_rows, extent = row_factors.shape
    rank = far_coupling.shape[-1]
    columns, col_rows = col_factors.shape[:2]
    probe_count = probes.shape[-1]
    parents = par_cols.shape[0]
    slots = near_blocks.shape[0]
    leaf_place = lax.axis_index("leaf")
    col_place = lax.axis_index("col")
    core = col_place % 2
    place = jnp.stack(
        [leaf_place // LEAF_Y, leaf_place % LEAF_Y, col_place // 2, core]
    ).astype(jnp.int32)

    all_columns, all_probes, all_rows, (upper, inverse) = gather_all(
        col_factors, probes, row_factors, place
    )
    triple = jax.ShapeDtypeStruct((3, extent, extent), F32)
    mine, away, updates = call(
        couple_kernel,
        [
            triple,
            triple,
            jax.ShapeDtypeStruct((columns, LEAF_Z * LEAF_Y * col_rows, rank), BF16),
        ],
        [],
        [*all_columns, far_coupling, par_coupling, col_transfer],
        [place, far_cols - col_place * columns, par_cols - col_place * (columns // 2)],
        [
            pltpu.VMEM((columns, extent, extent), F32),
            pltpu.VMEM((columns // 2, extent, extent), F32),
        ],
        14,
    )
    mine = (mine + sent(away, "col", flipped)).astype(BF16)
    across = [sent(mine, "col", along_x(by)) for by in (1, -1, 2)]
    [bundle] = call(
        leaf_kernel, [triple], [mine, *across], [upper, inverse, row_transfer], [place]
    )
    other = sent(bundle, "col", flipped)
    children = bundle[CHILD]
    same = sent(children, "leaf", flipped)
    width = 2 * COL_X
    cross = lax.ppermute(
        children,
        ("leaf", "col"),
        [(d, d // width % 2 * -width + (d // width + 1) % 2 * width + (d ^ 1)) for d in range(LEAF_Y * LEAF_Z * width)],
    )
    used = near_pattern[:, 0] >= 0
    row_local = jnp.where(used, near_pattern[:, 0] - leaf_place * leaves, 0)
    col_local = jnp.where(used, near_pattern[:, 1] - col_place * columns, 0)
    count = jnp.sum(used.astype(jnp.int32)).reshape(1)
    row_local, col_local = row_local.astype(jnp.int32), col_local.astype(jnp.int32)
    images = pl.pallas_call(
        near_kernel,
        grid_spec=pltpu.PrefetchScalarGridSpec(
            num_scalar_prefetch=4,
            grid=(1,),
            in_specs=[pl.BlockSpec(memory_space=pltpu.HBM) for _ in range(2)]
            + [pl.BlockSpec(memory_space=pltpu.VMEM)]
            + [pl.BlockSpec(memory_space=pltpu.HBM) for _ in all_rows],
            out_specs=whole((2, COL_X, leaves, local_rows, probe_count)),
            scratch_shapes=[
                pltpu.VMEM((leaves, 2 * COL_X * local_rows, probe_count), F32),
                pltpu.VMEM((leaves, rank, probe_count), F32),
                pltpu.VMEM(near_blocks.shape, BF16),
                pltpu.VMEM(all_probes.shape, BF16),
                pltpu.VMEM((len(all_rows),) + all_rows[0].shape, BF16),
                pltpu.SemaphoreType.DMA((slots,)),
                pltpu.SemaphoreType.DMA((1 + len(all_rows),)),
            ],
        ),
        out_shape=jax.ShapeDtypeStruct((2, COL_X, leaves, local_rows, probe_count), BF16),
        compiler_params=pltpu.CompilerParams(vmem_limit_bytes=26 << 20),
        name="near_kernel",
    )(
        place,
        row_local,
        col_local,
        count,
        in_hbm(near_blocks),
        in_hbm(all_probes),
        in_vmem(updates),
        *[in_hbm(piece) for piece in all_rows],
    )
    near_sent, near_own = scatter_start(images, col_place // 2, core)
    other, same, cross, *near_sent = lax.optimization_barrier((other, same, cross, *near_sent))
    near_image = near_own
    for by, piece in zip((1, -1, 2), near_sent):
        near_image = near_image + sent(piece, "col", along_x(by)).astype(F32)
    parent_transfer, new_basis = call(
        parent_kernel,
        [
            jax.ShapeDtypeStruct((parents, rank, extent), F32),
            jax.ShapeDtypeStruct((leaves, local_rows, rank), BF16),
        ],
        [bundle, other, same, cross],
        [row_factors],
        [place],
    )

    return (new_basis, jnp.swapaxes(parent_transfer, 1, 2), near_image)


def solution(mesh):
    placed = (
        P("leaf", "col", None),
        P("col", "leaf", None),
        P("leaf", "col"),
        P("leaf", "col", None, None),
        P("leaf", None, None),
        P("col", None, None),
        P("leaf", "col"),
        P("leaf", "col", None, None),
        P(("leaf", "col"), None),
        P(("leaf", "col"), None, None),
        P("col", "leaf", None),
    )
    return jax.shard_map(
        on_device,
        mesh=mesh,
        in_specs=placed,
        out_specs=(P("leaf", "col", None), P("leaf", None, None), P("leaf", "col", None)),
        check_vma=False,
    )
```

```python
import functools

import jax
import jax.numpy as jnp
from jax import lax
from jax.experimental import pallas as pl
from jax.experimental.pallas import tpu as pltpu
from jax.sharding import PartitionSpec as P

SWEEPS = 3
TILE = 8
LEAF_Y = 4
LEAF_Z = 8
COL_X = 4
PLACES_Z = (0, -1, 1, -2, 2, -3, 3, 4)
PLACES_Y = (0, 1, 2, -1)
PLACES_X = (0, -1, 1, 2)
Z, Y, X, CORE = range(4)
CHILD, COEFFICIENT, WEIGHT = range(3)
F32 = jnp.float32
BF16 = jnp.bfloat16

NN = (((1,), (0,)), ((), ()))
NT = (((1,), (1,)), ((), ()))
TN = (((0,), (0,)), ((), ()))


def dot(left, right, dims=NN):
    return lax.dot_general(left, right, dims, preferred_element_type=F32)


def halves(value):
    high = value.astype(BF16)
    return high, (value - high.astype(F32)).astype(BF16)


def dot_wide(left, right, dims=NN):
    left_high, left_low = halves(left)
    right_high, right_low = halves(right)
    return (
        dot(left_high, right_high, dims)
        + dot(left_high, right_low, dims)
        + dot(left_low, right_high, dims)
    )


def dot_exact_left(left, right, dims=NN):
    high, low = halves(right)
    return dot(left, high, dims) + dot(left, low, dims)


def dot_exact_right(left, right, dims=NN):
    high, low = halves(left)
    return dot(high, right, dims) + dot(low, right, dims)


def eliminate(systems, block=TILE):
    order = systems[0][0].shape[0]
    lanes = systems[0][0].shape[1]
    count = order // TILE
    inside = lax.broadcasted_iota(jnp.int32, (TILE, lanes), 0)

    def over_lanes(tile, lane):
        return jnp.broadcast_to(tile[:, lane : lane + 1], (TILE, lanes))

    def over_rows(tile, row):
        return jnp.broadcast_to(tile[row : row + 1], (TILE, lanes))

    work = [
        [[m[r * TILE : (r + 1) * TILE] for r in range(count)] for m in system]
        for system in systems
    ]
    span = range(block)
    for first in range(0, order, block):
        at, row = divmod(first, TILE)
        for parts in work:
            lead = parts[0]
            pivots = [over_lanes(lead[at], first + i) for i in span]
            d = [[over_rows(pivots[i], row + r) if r >= i else None for i in span] for r in span]
            roots = []
            for i in span:
                root = lax.rsqrt(d[i][i])
                roots.append(root)
                for r in range(i + 1, block):
                    d[r][i] = d[r][i] * root
                    for s in range(i + 1, r + 1):
                        d[r][s] = d[r][s] - d[r][i] * d[s][i]
            solved = []
            for part in parts:
                forward = []
                for i in span:
                    value = over_rows(part[at], row + i)
                    for m in range(i):
                        value = value - d[i][m] * forward[m]
                    forward.append(value * roots[i])
                backward = [None] * block
                for i in reversed(span):
                    value = forward[i]
                    for m in range(i + 1, block):
                        value = value - d[m][i] * backward[m]
                    backward[i] = value * roots[i]
                solved.append((forward, backward))
            for r in range(at, count):
                if r == at and row + block == TILE:
                    continue
                factors = [over_lanes(lead[r], first + i) for i in span]
                if r == at:
                    factors = [jnp.where(inside >= row + block, f, 0.0) for f in factors]
                for part, (_, backward) in zip(parts, solved):
                    for f, b in zip(factors, backward):
                        part[r] = part[r] - f * b
            for part, (forward, _) in zip(parts, solved):
                for i in span:
                    part[at] = jnp.where(inside == row + i, forward[i], part[at])
    return [[jnp.concatenate(part, axis=0) for part in parts] for parts in work]


def eye(order):
    rows = lax.broadcasted_iota(jnp.int32, (order, order), 0)
    cols = lax.broadcasted_iota(jnp.int32, (order, order), 1)
    return jnp.where(rows == cols, 1.0, 0.0).astype(F32)


def factor_kernel(place_ref, *refs):
    pieces = refs[: len(PLACES_X)]
    upper_ref, inverse_ref = refs[len(PLACES_X) :]
    leaves, extent = upper_ref.shape[0], upper_ref.shape[1]
    cores, local = pieces[0].shape[0], pieces[0].shape[2]
    half = extent // 2
    grams = []
    for t in range(leaves):
        leaf = place_ref[CORE] * leaves + t
        rows = jnp.concatenate(
            [p[:, leaf].reshape(cores * local, extent) for p in pieces], axis=0
        )
        grams.append(dot(rows, rows, TN))
    unit, blank = eye(half), jnp.zeros((half, half), F32)
    firsts = eliminate(
        [[g[:half], jnp.concatenate([unit, blank], axis=1)] for g in grams]
    )
    seconds = eliminate(
        [
            [
                jnp.concatenate(
                    [g[half:, half:] - dot_wide(f[0][:, half:], f[0][:, half:], TN), unit],
                    axis=1,
                )
            ]
            for g, f in zip(grams, firsts)
        ]
    )
    above = lax.broadcasted_iota(jnp.int32, (half, extent), 1) >= lax.broadcasted_iota(
        jnp.int32, (half, extent), 0
    )
    for t in range(leaves):
        first, first_inverse = firsts[t][0], firsts[t][1][:, :half]
        second, second_inverse = seconds[t][0][:, :half], seconds[t][0][:, half:]
        upper_ref[t, :half] = jnp.where(above, first, 0.0)
        upper_ref[t, half:, :half] = blank
        upper_ref[t, half:, half:] = jnp.where(above[:, :half], second, 0.0)
        inverse_ref[t, :half, :half] = first_inverse
        inverse_ref[t, :half, half:] = blank
        inverse_ref[t, half:, :half] = -dot_wide(
            second_inverse, dot_wide(first[:, half:], first_inverse, TN)
        )
        inverse_ref[t, half:, half:] = second_inverse


def couple_sum(couplings, grams):
    half = couplings[0].shape[0]
    stacked = jnp.concatenate(couplings, axis=1)
    right = jnp.concatenate(
        [
            jnp.concatenate(
                [dot_exact_right(p[:half, :half], s, NT), p[:half, half:]], axis=1
            )
            for s, p in zip(couplings, grams)
        ],
        axis=0,
    )
    upper = dot_exact_left(stacked, right)
    lower_right = functools.reduce(jnp.add, [p[half:, half:] for p in grams])
    return upper[:, :half], upper[:, half:], lower_right


def couple_kernel(place_ref, far_ref, par_ref, *refs):
    own_ref, left_ref, right_ref, early_ref, late_ref = refs[:5]
    far_coupling_ref, par_coupling_ref, transfer_ref = refs[5:8]
    mine_ref, away_ref, update_ref, gram_ref, parent_ref = refs[8:]
    columns, rank = transfer_ref.shape[0], transfer_ref.shape[1]
    leaves, far_row = far_coupling_ref.shape[0], far_coupling_ref.shape[1]
    parents, par_row = par_coupling_ref.shape[0], par_coupling_ref.shape[1]
    around, local = own_ref.shape[0], own_ref.shape[2]
    pieces = [own_ref, left_ref, right_ref, early_ref, late_ref]
    offsets = (0, -1, 1, 2, 2)
    starts = (0, 0, 0, 0, around // 2)
    for s in range(columns):
        slab = jnp.concatenate(
            [p[:, s].reshape(p.shape[0] * local, 2 * rank) for p in pieces], axis=0
        )
        gram_ref[s] = dot(slab, slab, TN)
    for piece, off_y, start in zip(pieces, offsets, starts):
        y = (place_ref[Y] + off_y + LEAF_Y) % LEAF_Y
        for i in range(piece.shape[0]):
            z = (place_ref[Z] + PLACES_Z[start + i] + LEAF_Z) % LEAF_Z
            at = pl.multiple_of((z * LEAF_Y + y) * local, local)
            for s in range(columns):
                update_ref[s, pl.ds(at, local), :] = piece[i, s, :, rank:]
    for q in range(columns // 2):
        group, inner = divmod(q, leaves)
        child = 2 * group * leaves + inner
        total = None
        for c in (child, child + leaves):
            gram, transfer = gram_ref[c], transfer_ref[c]
            upper = dot_exact_left(transfer, gram[:rank], TN)
            lifted = (
                dot_exact_right(upper[:, :rank], transfer),
                upper[:, rank:],
                gram[rank:, rank:],
            )
            total = lifted if total is None else tuple(a + b for a, b in zip(total, lifted))
        parent_ref[q, :rank, :rank] = total[0]
        parent_ref[q, :rank, rank:] = total[1]
        parent_ref[q, rank:, rank:] = total[2]
    core = place_ref[CORE]
    each = leaves // 2
    for out_ref, side in ((mine_ref, core), (away_ref, 1 - core)):
        jobs = [
            (t, far_coupling_ref, far_ref, gram_ref, side * each + t, far_row)
            for t in range(each)
        ]
        jobs.append((each, par_coupling_ref, par_ref, parent_ref, side, par_row))
        for out, coupling_ref, cols_ref, source_ref, t, width in jobs:
            upper_left, crosswise, lower_right = couple_sum(
                [coupling_ref[t, k] for k in range(width)],
                [source_ref[cols_ref[t, k]] for k in range(width)],
            )
            out_ref[out, :rank, :rank] = upper_left
            out_ref[out, :rank, rank:] = crosswise
            out_ref[out, rank:, :rank] = crosswise.T
            out_ref[out, rank:, rank:] = lower_right


def leading(matrices, rank):
    extent = matrices[0].shape[0]
    scaled = []
    on_diagonal = eye(extent)
    for matrix in matrices:
        diagonal = jnp.sum(matrix * on_diagonal, axis=0, keepdims=True)
        trace = jnp.sum(diagonal, axis=1, keepdims=True)
        scaled.append(matrix * (extent / trace))
    current = [s[:rank] for s in scaled]
    for sweep in range(SWEEPS):
        if sweep:
            current = [dot_wide(c, s) for c, s in zip(current, scaled)]
        blank = jnp.zeros((rank, extent - rank), F32)
        systems = [
            [jnp.concatenate([dot_wide(c, c, NT), blank], axis=1), c] for c in current
        ]
        current = [parts[1] for parts in eliminate(systems)]
    return current


def leaf_kernel(
    place_ref, mine_ref, left_ref, right_ref, across_ref, upper_ref, inverse_ref, transfer_ref, out_ref
):
    leaves, extent = upper_ref.shape[0], upper_ref.shape[1]
    rank = transfer_ref.shape[1]

    def summed(at):
        near = mine_ref[at].astype(F32) + across_ref[at].astype(F32)
        return near + (left_ref[at].astype(F32) + right_ref[at].astype(F32))

    whitened = []
    for t in range(leaves):
        upper = upper_ref[t]
        whitened.append(dot_wide(dot_wide(upper, summed(t)), upper, NT))
    spaces = leading(whitened, rank)
    for t in range(leaves):
        space = spaces[t]
        child = dot_wide(space, upper_ref[t])
        transfer = transfer_ref[place_ref[CORE] * leaves + t]
        rows = pl.ds(t * rank, rank)
        out_ref[CHILD, rows, :rank] = dot_exact_right(child[:, :rank], transfer)
        out_ref[CHILD, rows, rank:] = child[:, rank:]
        out_ref[COEFFICIENT, rows, :] = dot_wide(space, inverse_ref[t])
    out_ref[WEIGHT] = summed(leaves)


def parent_kernel(
    place_ref, own_ref, other_ref, same_ref, cross_ref, rows_ref, out_ref, basis_ref
):
    parents, rank, extent = out_ref.shape
    core, odd = place_ref[CORE], place_ref[Y] % 2
    kept = jnp.where(core == odd, own_ref[CHILD], other_ref[CHILD])
    incoming = jnp.where(core == odd, same_ref[...], cross_ref[...])
    first = jnp.where(odd == 0, kept, incoming)
    second = jnp.where(odd == 0, incoming, kept)
    matrices = []
    for p in range(parents):
        rows = slice(p * rank, (p + 1) * rank)
        stacked = jnp.concatenate([first[rows], second[rows]], axis=0)
        weight = jnp.where(core == p, own_ref[WEIGHT], other_ref[WEIGHT])
        matrices.append(dot_wide(dot_wide(stacked, weight), stacked, NT))
    for p, space in enumerate(leading(matrices, rank)):
        out_ref[p] = space
    for ref, side in ((own_ref, core), (other_ref, 1 - core)):
        for t in range(parents):
            coefficient = ref[COEFFICIENT, t * rank : (t + 1) * rank].astype(BF16)
            leaf = side * parents + t
            basis_ref[leaf] = dot(rows_ref[leaf], coefficient, NT).astype(BF16)


def near_kernel(place_ref, row_ref, col_ref, count_ref, blocks_ref, *refs):
    probes_from, update_ref, pieces_from, out_ref = refs[0], refs[1], refs[2:6], refs[6]
    total_ref, proj_ref, block_ref, probe_ref, pieces_ref = refs[7:12]
    block_semaphores, semaphores = refs[12:]
    slots = block_ref.shape[0]
    cores, leaves, local, extent = pieces_from[0].shape
    rank = extent // 2
    live = count_ref[0]
    def block_copy(k):
        return pltpu.make_async_copy(
            blocks_ref.at[k], block_ref.at[k], block_semaphores.at[k]
        )

    copies = [pltpu.make_async_copy(probes_from, probe_ref, semaphores.at[0])]
    for i, piece in enumerate(pieces_from):
        copies.append(pltpu.make_async_copy(piece, pieces_ref.at[i], semaphores.at[i + 1]))
    for copy in copies:
        copy.start()
    for k in range(slots):
        @pl.when(k < live)
        def _():
            block_copy(k).start()
    total_ref[...] = jnp.zeros_like(total_ref)
    proj_ref[...] = jnp.zeros_like(proj_ref)
    for copy in copies:
        copy.wait()

    def slot(k, carry):
        block_copy(k).wait()
        row, col = row_ref[k], col_ref[k]
        probe = jnp.concatenate(
            [
                probe_ref[z, (y - place_ref[Y] + LEAF_Y) % LEAF_Y, col]
                for z in range(LEAF_Z)
                for y in range(LEAF_Y)
            ],
            axis=0,
        )
        total_ref[row] += dot(block_ref[k], probe)
        proj_ref[row] += dot(update_ref[col], probe, TN)
        return carry

    lax.fori_loop(0, live, slot, 0)
    for i in range(len(pieces_from)):
        x = (place_ref[X] + PLACES_X[i] + COL_X) % COL_X
        for flip in range(cores):
            core = (place_ref[CORE] + flip) % 2
            at = pl.multiple_of((x * 2 + core) * local, local)
            for t in range(leaves):
                updated = total_ref[t, pl.ds(at, local), :] + dot_exact_left(
                    pieces_ref[i, flip, t, :, rank:], proj_ref[t]
                )
                out_ref[core, x, t] = updated.astype(BF16)


def whole(shape):
    return pl.BlockSpec(shape, lambda *_: (0,) * len(shape))


def in_hbm(array):
    return pltpu.with_memory_space_constraint(array, pltpu.HBM)


def in_vmem(array):
    return pltpu.with_memory_space_constraint(array, pltpu.VMEM)


def call(body, outs, near, far=(), scalars=(), scratch=(), room=8):
    before, held, inner = len(scalars), len(near), len(far)
    last = before + held + inner + len(outs) + len(scratch)

    def fetched(*refs):
        named, sources = refs[: before + held], refs[before + held : before + held + inner]
        made, targets = refs[before + held + inner : last], refs[last : last + inner]
        copies = [
            pltpu.make_async_copy(source, target, refs[-1].at[i])
            for i, (source, target) in enumerate(zip(sources, targets))
        ]
        for copy in copies:
            copy.start()
        for copy in copies:
            copy.wait()
        body(*named, *targets, *made)

    return pl.pallas_call(
        fetched if inner else body,
        grid_spec=pltpu.PrefetchScalarGridSpec(
            num_scalar_prefetch=before,
            grid=(1,),
            in_specs=[pl.BlockSpec(memory_space=pltpu.VMEM) for _ in near]
            + [pl.BlockSpec(memory_space=pltpu.HBM) for _ in far],
            out_specs=[whole(o.shape) for o in outs],
            scratch_shapes=[
                *scratch,
                *[pltpu.VMEM(a.shape, a.dtype) for a in far],
                *([pltpu.SemaphoreType.DMA((inner,))] if inner else []),
            ],
        ),
        out_shape=outs,
        compiler_params=pltpu.CompilerParams(vmem_limit_bytes=room << 20),
        name=body.__name__,
    )(*scalars, *[in_vmem(a) for a in near], *[in_hbm(a) for a in far])


def sent(value, axis, target):
    count = lax.axis_size(axis)
    return lax.ppermute(value, axis, [(d, target(d)) for d in range(count)])


def along_y(by):
    return lambda d: d // LEAF_Y * LEAF_Y + (d + by) % LEAF_Y


def along_z(by):
    return lambda d: (d + by * LEAF_Y) % (LEAF_Y * LEAF_Z)


def along_x(by):
    return lambda d: (d + 2 * by) % (2 * COL_X)


def flipped(d):
    return d ^ 1


def gather_all(columns, probes, rows, place):
    moved = [sent(probes, "leaf", along_y(-y)) for y in PLACES_Y[1:]]
    start = jnp.stack([probes] + moved)
    groups = [[z * LEAF_Y + y for z in range(LEAF_Z)] for y in range(LEAF_Y)]
    all_probes = lax.all_gather(start, "leaf", axis=0, axis_index_groups=groups)
    columns, _ = lax.optimization_barrier((columns, moved[0]))
    own = jnp.stack([columns] + [sent(columns, "leaf", along_z(-z)) for z in PLACES_Z[1:]])
    pair = jnp.stack([rows, sent(rows, "col", flipped)])
    own, pair = lax.optimization_barrier((own, pair))
    left = sent(own, "leaf", along_y(1))
    right = sent(own, "leaf", along_y(-1))
    all_rows = [pair] + [sent(pair, "col", along_x(-x)) for x in PLACES_X[1:]]
    left, right, *all_rows = lax.optimization_barrier((left, right, *all_rows))
    half = own.shape[0] // 2
    early = sent(left[:half], "leaf", along_y(1))
    late = sent(right[half:], "leaf", along_y(-1))
    leaves, extent = rows.shape[0], rows.shape[2]
    square = jax.ShapeDtypeStruct((leaves // 2, extent, extent), F32)
    factors = call(factor_kernel, [square, square], all_rows, (), [place])
    own, left, right, early, late, *factors = lax.optimization_barrier(
        (own, left, right, early, late, *factors)
    )
    return (own, left, right, early, late), all_probes, all_rows, factors


def scatter_start(parts, place, core):
    away = lax.dynamic_index_in_dim(parts, 1 - core, 0, keepdims=False)
    mine = lax.dynamic_index_in_dim(parts, core, 0, keepdims=False)
    paired = mine.astype(F32) + sent(away, "col", flipped).astype(F32)
    narrow = paired.astype(BF16)
    own = lax.dynamic_index_in_dim(paired, place, 0, keepdims=False)
    pieces = [
        lax.dynamic_index_in_dim(narrow, (place + by) % COL_X, 0, keepdims=False)
        for by in (1, -1, 2)
    ]
    return pieces, own


def on_device(
    row_factors,
    col_factors,
    far_cols,
    far_coupling,
    row_transfer,
    col_transfer,
    par_cols,
    par_coupling,
    near_pattern,
    near_blocks,
    probes,
):
    leaves, local_rows, extent = row_factors.shape
    rank = far_coupling.shape[-1]
    columns, col_rows = col_factors.shape[:2]
    probe_count = probes.shape[-1]
    parents = par_cols.shape[0]
    slots = near_blocks.shape[0]
    leaf_place = lax.axis_index("leaf")
    col_place = lax.axis_index("col")
    core = col_place % 2
    place = jnp.stack(
        [leaf_place // LEAF_Y, leaf_place % LEAF_Y, col_place // 2, core]
    ).astype(jnp.int32)

    all_columns, all_probes, all_rows, (upper, inverse) = gather_all(
        col_factors, probes, row_factors, place
    )
    triple = jax.ShapeDtypeStruct((3, extent, extent), F32)
    mine, away, updates = call(
        couple_kernel,
        [
            triple,
            triple,
            jax.ShapeDtypeStruct((columns, LEAF_Z * LEAF_Y * col_rows, rank), BF16),
        ],
        [],
        [*all_columns, far_coupling, par_coupling, col_transfer],
        [place, far_cols - col_place * columns, par_cols - col_place * (columns // 2)],
        [
            pltpu.VMEM((columns, extent, extent), F32),
            pltpu.VMEM((columns // 2, extent, extent), F32),
        ],
        14,
    )
    mine = (mine + sent(away, "col", flipped)).astype(BF16)
    across = [sent(mine, "col", along_x(by)) for by in (1, -1, 2)]
    used = near_pattern[:, 0] >= 0
    row_local = jnp.where(used, near_pattern[:, 0] - leaf_place * leaves, 0)
    col_local = jnp.where(used, near_pattern[:, 1] - col_place * columns, 0)
    count = jnp.sum(used.astype(jnp.int32)).reshape(1)
    row_local, col_local = row_local.astype(jnp.int32), col_local.astype(jnp.int32)
    row_local, col_local, count, *_ = lax.optimization_barrier(
        (row_local, col_local, count, *across)
    )
    images = pl.pallas_call(
        near_kernel,
        grid_spec=pltpu.PrefetchScalarGridSpec(
            num_scalar_prefetch=4,
            grid=(1,),
            in_specs=[pl.BlockSpec(memory_space=pltpu.HBM) for _ in range(2)]
            + [pl.BlockSpec(memory_space=pltpu.VMEM)]
            + [pl.BlockSpec(memory_space=pltpu.HBM) for _ in all_rows],
            out_specs=whole((2, COL_X, leaves, local_rows, probe_count)),
            scratch_shapes=[
                pltpu.VMEM((leaves, 2 * COL_X * local_rows, probe_count), F32),
                pltpu.VMEM((leaves, rank, probe_count), F32),
                pltpu.VMEM(near_blocks.shape, BF16),
                pltpu.VMEM(all_probes.shape, BF16),
                pltpu.VMEM((len(all_rows),) + all_rows[0].shape, BF16),
                pltpu.SemaphoreType.DMA((slots,)),
                pltpu.SemaphoreType.DMA((1 + len(all_rows),)),
            ],
        ),
        out_shape=jax.ShapeDtypeStruct((2, COL_X, leaves, local_rows, probe_count), BF16),
        compiler_params=pltpu.CompilerParams(vmem_limit_bytes=26 << 20),
        name="near_kernel",
    )(
        place,
        row_local,
        col_local,
        count,
        in_hbm(near_blocks),
        in_hbm(all_probes),
        in_vmem(updates),
        *[in_hbm(piece) for piece in all_rows],
    )
    [bundle] = call(
        leaf_kernel, [triple], [], [mine, *across, upper, inverse, row_transfer], [place]
    )
    other = sent(bundle, "col", flipped)
    children = bundle[CHILD]
    same = sent(children, "leaf", flipped)
    width = 2 * COL_X
    cross = lax.ppermute(
        children,
        ("leaf", "col"),
        [(d, d // width % 2 * -width + (d // width + 1) % 2 * width + (d ^ 1)) for d in range(LEAF_Y * LEAF_Z * width)],
    )
    near_sent, near_own = scatter_start(images, col_place // 2, core)
    other, same, cross, *near_sent = lax.optimization_barrier((other, same, cross, *near_sent))
    near_image = near_own
    for by, piece in zip((1, -1, 2), near_sent):
        near_image = near_image + sent(piece, "col", along_x(by)).astype(F32)
    parent_transfer, new_basis = call(
        parent_kernel,
        [
            jax.ShapeDtypeStruct((parents, rank, extent), F32),
            jax.ShapeDtypeStruct((leaves, local_rows, rank), BF16),
        ],
        [bundle, other, same, cross],
        [row_factors],
        [place],
    )

    return (new_basis, jnp.swapaxes(parent_transfer, 1, 2), near_image)


def solution(mesh):
    placed = (
        P("leaf", "col", None),
        P("col", "leaf", None),
        P("leaf", "col"),
        P("leaf", "col", None, None),
        P("leaf", None, None),
        P("col", None, None),
        P("leaf", "col"),
        P("leaf", "col", None, None),
        P(("leaf", "col"), None),
        P(("leaf", "col"), None, None),
        P("col", "leaf", None),
    )
    return jax.shard_map(
        on_device,
        mesh=mesh,
        in_specs=placed,
        out_specs=(P("leaf", "col", None), P("leaf", None, None), P("leaf", "col", None)),
        check_vma=False,
    )
```
